32 devices in a mesh: main: 4 (over y, core), sub: 8 (over z, x).
Axes of the slice: x: 2, y: 2, z: 4, core: 2. Of those that a mesh axis runs over, the one named last changes fastest.
Arguments:
- byte_states: bfloat16 [16384, 1024], P(('main', 'sub')), may hold values from -8 to 8
- boundary_flags: int32 [16384], P(('main', 'sub')), may hold values from 0 to 1, as said below
- span_counts: int32 [32], replicated, may hold values from 2 to 96, as said below
- enc_norm_gain: float32 [1024], replicated, may hold values from 0.5 to 1.5
- mamba_in: bfloat16 [1024, 4096], replicated, may hold values from -0.1875 to 0.1875
- mamba_bc: bfloat16 [1024, 256], replicated, may hold values from -0.03125 to 0.03125
- mamba_dt: bfloat16 [1024, 32], replicated, may hold values from -0.1875 to 0.1875
- dt_bias: float32 [32], replicated, may hold values from -3 to 0.5
- decay_rate: float32 [32], replicated, may hold values from 0.00024414062 to 0.1
- skip_gain: float32 [32], replicated, may hold values from 1 to 10
- gate_norm_gain: float32 [2048], replicated, may hold values from 0.5 to 1.5
- mamba_out: bfloat16 [2048, 1024], replicated, may hold values from -0.125 to 0.125
- down_proj: bfloat16 [1024, 2048], replicated, may hold values from -0.1875 to 0.1875
- attn_norm_gain: float32 [2048], replicated, may hold values from 0.5 to 1.5
- qkv_weight: bfloat16 [2048, 16, 384], P(None, 'sub'), may hold values from -8 to 8
- out_weight: bfloat16 [16, 128, 2048], P('sub'), may hold values from -0.125 to 0.125
- up_proj: bfloat16 [2048, 1024], replicated, may hold values from -0.125 to 0.125
Outputs:
- byte_out: bfloat16 [16384, 1024], P(('main', 'sub'))
The draws below stay inside these ranges and needn't reach their ends.
Inputs may be any that keep to these rules, and one draw needn't show every extreme that they name: `boundary_flags`: each device's block of 512 bytes holds between 2 and 96 flagged bytes, and some block holds exactly 96; the first byte of the sequence is flagged. span_counts[d] is the number of flagged bytes in block d.
All inputs are finite; a program needn't handle non-finite values.
Results may differ from the reference program's by a relative error of at most 0.012.
Values may be sent and summed in bfloat16 or wider, within the bound.
No kernel may reach another device: no remote copies, remote signals or barrier semaphores. Data moves between devices by JAX's collectives and lax.ppermute only.
A program may use at most 384 MiB of HBM per device.

```python
import math
import jax
import jax.numpy as jnp
from jax import lax

DB = 1024
INNER_WIDTH = 2048
SCAN_HEAD_COUNT = 32
SCAN_HEAD_WIDTH = 64
SCAN_STATE_SIZE = 128
DM = 2048
HEADS = 16
HD = 128
BLOCK = 64
BYTES_DEV = 512
CAP = 96
NDEV = 32
BYTES = 16384
SLOTS = 3072
N_SUB = 8


def boundary_table(key):
    base = jax.random.fold_in(key, 7)
    count_key, perm_key, full_key = jax.random.split(base, 3)
    counts = jax.random.randint(count_key, (NDEV,), 2, CAP + 1)
    full_device = jax.random.randint(full_key, (), 1, NDEV)
    counts = jnp.where(jnp.arange(NDEV) == full_device, CAP, counts)
    counts = counts.at[0].set(jnp.minimum(counts[0], CAP - 1))
    perms = jax.vmap(lambda single: jax.random.permutation(single, BYTES_DEV))(jax.random.split(perm_key, NDEV))
    inverse = jnp.argsort(perms, axis=1, stable=True)
    flags = (inverse < counts[:, None]).astype(jnp.int32)
    flags = flags.at[0, 0].set(1)
    return (flags.reshape(BYTES).astype(jnp.int32), jnp.sum(flags, 1).astype(jnp.int32))


def draw_boundary_flags(key, part):
    return boundary_table(key)[0]


def draw_span_counts(key, part):
    return boundary_table(key)[1]


def draw_byte_states(key, part):
    noise_key = jax.random.fold_in(jax.random.fold_in(key, 11), 0)
    block_key = jax.random.fold_in(jax.random.fold_in(key, 11), 2)
    noise = jax.random.normal(noise_key, (BYTES, DB), jnp.float32)
    block_vec = jax.random.uniform(block_key, (NDEV, 1, DB), jnp.float32, -1.5, 1.5)
    values = jnp.clip(noise, -6.0, 6.0)
    values = (values.reshape(NDEV, BYTES_DEV, DB) + block_vec).reshape(BYTES, DB)
    return values.astype(jnp.bfloat16)


def draw_qkv_weight(key, part):
    base_key = jax.random.fold_in(jax.random.fold_in(key, 13), 0)
    values = jnp.clip(jax.random.normal(base_key, (DM, HEADS, 3 * HD), jnp.float32), -4.0, 4.0) * DM ** (-0.5)
    return values.astype(jnp.bfloat16)


def block_levels(stream_key, extent, shards, least, top_value):
    level = 1.0
    for dim, shards_of in shards:
        heights = jax.random.uniform(jax.random.fold_in(jax.random.fold_in(stream_key, 6), dim), (shards_of,), jnp.float32, least / len(shards), top_value / len(shards))
        level = level * jnp.repeat(jnp.exp(heights), extent[dim] // shards_of).reshape((-1,) + (1,) * (len(extent) - 1 - dim))
    return level


def bell_draw(stream_key, extent, scale, most, cuts=(), kind=jnp.bfloat16):
    level = block_levels(stream_key, extent, cuts, -0.22, 0.18) if cuts else 1.0
    values = jax.random.normal(stream_key, extent, jnp.float32) * scale * level
    return jnp.minimum(jnp.maximum(values, -most), most).astype(kind)


def setup_inputs(seed: int = 0) -> dict:
    seeds = jax.random.split(jax.random.key(seed), 18)
    return {
        "byte_states": draw_byte_states(jax.random.fold_in(seeds[17], 71), 0),
        "boundary_flags": draw_boundary_flags(jax.random.fold_in(seeds[17], 71), 0),
        "span_counts": draw_span_counts(jax.random.fold_in(seeds[17], 71), 0),
        "enc_norm_gain": jnp.clip(1.0 + 0.1 * jax.random.normal(seeds[3], (DB,), jnp.float32), 0.5, 1.5),
        "mamba_in": bell_draw(seeds[4], (DB, 2 * INNER_WIDTH), DB ** -0.5, 0.1875),
        "mamba_bc": bell_draw(seeds[5], (DB, 2 * SCAN_STATE_SIZE), (DB * SCAN_STATE_SIZE // 4) ** -0.5, 0.03125),
        "mamba_dt": bell_draw(seeds[6], (DB, SCAN_HEAD_COUNT), DB ** -0.5, 0.1875),
        "dt_bias": jnp.clip(jax.random.uniform(seeds[7], (SCAN_HEAD_COUNT,), jnp.float32, -3.0, 0.5), -3.0, 0.5),
        "decay_rate": jnp.clip(jnp.exp(jax.random.uniform(seeds[8], (SCAN_HEAD_COUNT,), jnp.float32, math.log(0.00024414062), math.log(0.1))), 0.00024414062, 0.1),
        "skip_gain": jnp.clip(jnp.exp(jax.random.uniform(seeds[9], (SCAN_HEAD_COUNT,), jnp.float32, math.log(1.0), math.log(10.0))), 1.0, 10.0),
        "gate_norm_gain": jnp.clip(1.0 + 0.1 * jax.random.normal(seeds[10], (INNER_WIDTH,), jnp.float32), 0.5, 1.5),
        "mamba_out": bell_draw(seeds[11], (INNER_WIDTH, DB), INNER_WIDTH ** -0.5, 0.125),
        "down_proj": bell_draw(seeds[12], (DB, DM), DB ** -0.5, 0.1875),
        "attn_norm_gain": jnp.clip(1.0 + 0.1 * jax.random.normal(seeds[13], (DM,), jnp.float32), 0.5, 1.5),
        "qkv_weight": draw_qkv_weight(jax.random.fold_in(seeds[17], 71), 0),
        "out_weight": bell_draw(seeds[15], (HEADS, HD, DM), DM ** -0.5, 0.125, ((0, 8),)),
        "up_proj": bell_draw(seeds[16], (DM, DB), DM ** -0.5, 0.125),
    }


epsilon = 1e-06
highest = lax.Precision.HIGHEST

def rms_norm(values, gain):
    return values * lax.rsqrt(lax.optimization_barrier(jnp.mean(values * values, -1, keepdims=True)) + epsilon) * gain

def block_scan(inputs, initial):
    input_portion, b_rows, c_rows, log_step, dt_rows = inputs
    length, head_count, head_width = input_portion.shape
    block_count = length // BLOCK
    causal = jnp.arange(BLOCK)[:, None] >= jnp.arange(BLOCK)[None, :]

    def advance(carried_in, pieces):
        memory, offset = carried_in
        x_block, b_block, c_block, log_block, dt_block = pieces
        cumulative = jnp.cumsum(log_block, 0)
        contact = jnp.dot(c_block, b_block.T, precision=highest)
        log_gap = cumulative[:, None, :] - cumulative[None, :, :]
        weights = jnp.where(causal[:, :, None], jnp.exp(jnp.where(causal[:, :, None], log_gap, 0.0)), 0.0)
        weights = weights * contact[:, :, None] * dt_block[None, :, :]
        within = jnp.einsum('tsh,shp->thp', weights, x_block, precision=highest)
        carried = jnp.exp(cumulative)[:, :, None] * jnp.einsum('tn,hpn->thp', c_block, memory, precision=highest)
        tail_weight = jnp.exp(cumulative[-1][None, :] - cumulative) * dt_block
        update = jnp.einsum('sh,shp,sn->hpn', tail_weight, x_block, b_block, precision=highest)
        new_memory = jnp.exp(cumulative[-1])[:, None, None] * memory + update
        return ((new_memory, offset + cumulative[-1]), (within + carried, cumulative + offset))
    pieces = (input_portion.reshape(block_count, BLOCK, head_count, head_width), b_rows.reshape(block_count, BLOCK, -1), c_rows.reshape(block_count, BLOCK, -1), log_step.reshape(block_count, BLOCK, head_count), dt_rows.reshape(block_count, BLOCK, head_count))
    (memory, decay_total), (scanned, cumulative) = lax.scan(advance, (initial, jnp.zeros((head_count,), jnp.float32)), pieces)
    return (scanned.reshape(length, head_count, head_width), cumulative.reshape(length, head_count), memory, decay_total)

def mamba_inputs(states, enc_norm_gain, mamba_in, mamba_bc, mamba_dt, dt_bias, decay_rate):
    normed = rms_norm(states.astype(jnp.float32), enc_norm_gain).astype(jnp.bfloat16)
    projected_input = jnp.dot(normed, mamba_in, preferred_element_type=jnp.float32)
    input_portion = jax.nn.silu(projected_input[:, :INNER_WIDTH]).reshape(-1, SCAN_HEAD_COUNT, SCAN_HEAD_WIDTH)
    gate_part = projected_input[:, INNER_WIDTH:]
    b_and_c = jnp.dot(normed, mamba_bc, preferred_element_type=jnp.float32)
    dt_rows = jax.nn.softplus(jnp.dot(normed, mamba_dt, preferred_element_type=jnp.float32) + dt_bias)
    log_step = -decay_rate * dt_rows
    return (input_portion, gate_part, b_and_c[:, :SCAN_STATE_SIZE], b_and_c[:, SCAN_STATE_SIZE:], log_step, dt_rows)

def finish(states, scanned, input_portion, gate_part, skip_gain, gate_norm_gain, mamba_out):
    gated = (scanned + skip_gain[None, :, None] * input_portion).reshape(-1, INNER_WIDTH) * jax.nn.silu(gate_part)
    gnorm = rms_norm(gated, gate_norm_gain).astype(jnp.bfloat16)
    mixed = jnp.dot(gnorm, mamba_out, preferred_element_type=jnp.float32)
    return (states.astype(jnp.float32) + mixed).astype(jnp.bfloat16)

def reference(byte_states, boundary_flags, span_counts, enc_norm_gain, mamba_in, mamba_bc, mamba_dt, dt_bias, decay_rate, skip_gain, gate_norm_gain, mamba_out, down_proj, attn_norm_gain, qkv_weight, out_weight, up_proj):
    per_device_blocks = byte_states.reshape(NDEV, BYTES_DEV, DB)

    def per_device_update(memory, states):
        input_portion, gate_part, b_rows, c_rows, log_step, dt_rows = mamba_inputs(states, enc_norm_gain, mamba_in, mamba_bc, mamba_dt, dt_bias, decay_rate)
        scanned, cumulative, memory, decay_total = block_scan((input_portion, b_rows, c_rows, log_step, dt_rows), memory)
        return (memory, finish(states, scanned, input_portion, gate_part, skip_gain, gate_norm_gain, mamba_out))
    unused_value, encoder_output = lax.scan(per_device_update, jnp.zeros((SCAN_HEAD_COUNT, SCAN_HEAD_WIDTH, SCAN_STATE_SIZE), jnp.float32), per_device_blocks)
    flags = boundary_flags.reshape(NDEV, BYTES_DEV)
    span_rank = (jnp.cumsum(flags, 1) - 1).astype(jnp.int32)
    slot_ids = jnp.arange(CAP, dtype=jnp.int32)
    picker = ((span_rank[:, None, :] == slot_ids[None, :, None]) & (flags[:, None, :] == 1)).astype(jnp.float32)
    span_rows = jnp.einsum('dcb,dbe->dce', picker, encoder_output.astype(jnp.float32)).astype(jnp.bfloat16)
    main_in = jnp.dot(span_rows.reshape(SLOTS, DB), down_proj, preferred_element_type=jnp.float32).astype(jnp.bfloat16)
    main_norm = rms_norm(main_in.astype(jnp.float32), attn_norm_gain).astype(jnp.bfloat16)
    projected_qkv = jnp.dot(main_norm, qkv_weight.reshape(DM, HEADS * 3 * HD), preferred_element_type=jnp.float32).astype(jnp.bfloat16)
    projected_qkv = projected_qkv.reshape(SLOTS, HEADS, 3 * HD).transpose(1, 0, 2)
    slot_pos = jnp.arange(SLOTS, dtype=jnp.int32)
    valid = slot_pos % CAP < jnp.take(span_counts, slot_pos // CAP)
    query_block = CAP * N_SUB
    score_scale = HD ** (-0.5)

    def one_head(head_qkv):
        queries = head_qkv[:, :HD]
        key_rows = head_qkv[:, HD:2 * HD]
        values = head_qkv[:, 2 * HD:]

        def one_block(first_row):
            row_block = lax.dynamic_slice_in_dim(queries, first_row, query_block, 0)
            scores = jnp.dot(row_block, key_rows.T, preferred_element_type=jnp.float32) * score_scale
            query_pos = first_row + jnp.arange(query_block, dtype=jnp.int32)
            allowed = (slot_pos[None, :] <= query_pos[:, None]) & valid[None, :]
            row_max = lax.optimization_barrier(jnp.max(jnp.where(allowed, scores, -1e+30), 1, keepdims=True))
            numer = jnp.where(allowed, jnp.exp(scores - row_max), 0.0)
            row_total = lax.optimization_barrier(jnp.sum(numer, 1, keepdims=True))
            mixed = jnp.dot(numer.astype(jnp.bfloat16), values, preferred_element_type=jnp.float32) / row_total
            return mixed.astype(jnp.bfloat16)
        starts = jnp.arange(SLOTS // query_block, dtype=jnp.int32) * query_block
        return lax.map(one_block, starts).reshape(SLOTS, HD)
    heads_out = lax.map(one_head, projected_qkv)
    attention = jnp.einsum('hsd,hde->se', heads_out.astype(jnp.float32), out_weight.astype(jnp.float32))
    main_out = (main_in.astype(jnp.float32) + attention).astype(jnp.bfloat16)
    span_up = jnp.dot(main_out, up_proj, preferred_element_type=jnp.float32).astype(jnp.bfloat16).reshape(NDEV, CAP, DB)
    device_ids = jnp.arange(NDEV, dtype=jnp.int32)
    last_row = span_up[device_ids, span_counts - 1].astype(jnp.float32)
    second_row = span_up[device_ids, span_counts - 2].astype(jnp.float32)
    zero_row = jnp.zeros((1, DB), jnp.float32)
    prev_last = jnp.concatenate([zero_row, last_row[:-1]], 0)
    prev_second = jnp.concatenate([zero_row, second_row[:-1]], 0)
    target = span_rank - 1
    spread = (target[:, :, None] == slot_ids[None, None, :]).astype(jnp.float32)
    upsampled = jnp.einsum('dbc,dce->dbe', spread, span_up.astype(jnp.float32))
    upsampled = upsampled + jnp.where((target == -1)[:, :, None], prev_last[:, None, :], 0.0)
    upsampled = upsampled + jnp.where((target == -2)[:, :, None], prev_second[:, None, :], 0.0)
    byte_out = (encoder_output.astype(jnp.float32) + upsampled).astype(jnp.bfloat16)
    return byte_out.reshape(BYTES, DB)
```

```python
import functools
import math

import jax
import jax.numpy as jnp
from jax import lax
from jax.experimental import pallas as pl
from jax.experimental.pallas import tpu as pltpu
from jax.sharding import PartitionSpec as P

INNER_WIDTH = 2048
HEAD_COUNT = 32
HEAD_WIDTH = 64
STATE = 128
HD = 128
CAP = 96
CHUNK = 128
LANES = 128
QUAD = 256
EXTRA = 16

epsilon = 1e-06
highest = lax.Precision.HIGHEST
LOG2E = math.log2(math.e)
BF = jnp.bfloat16
F32 = jnp.float32


def dot(a, b, **kw):
    return jnp.dot(a, b, preferred_element_type=F32, **kw)


def dot_t(a, b):
    return lax.dot_general(a, b, (((1,), (1,)), ((), ())), preferred_element_type=F32)


def silu(v):
    return v * jax.nn.sigmoid(v)


def params(**kw):
    return pltpu.CompilerParams(dimension_semantics=("arbitrary",), **kw)


def whole(shape):
    rank = len(shape)
    return pl.BlockSpec(shape, lambda j: (0,) * rank)


def pair_lanes(columns, pair):
    rows = columns.shape[0]
    low = jnp.broadcast_to(columns[:, 2 * pair : 2 * pair + 1], (rows, LANES))
    high = jnp.broadcast_to(columns[:, 2 * pair + 1 : 2 * pair + 2], (rows, LANES))
    lane = lax.broadcasted_iota(jnp.int32, (rows, LANES), 1)
    return jnp.where(lane < HEAD_WIDTH, low, high)


def quad_columns(table, j):
    return pltpu.roll(table, (LANES - 4 * j) % LANES, 1)


def states_body(
    bytes_ref, gain_ref, wx_ref, wbc_ref, wdt_ref, bias_ref, rate_ref,
    normed_ref, x_ref, bc_ref, cum_ref, late_ref, local_ref, decay_ref, send_ref,
    bt_ref, weight_ref, total_ref,
):
    j = pl.program_id(0)
    rows = bytes_ref.shape[0]
    chunks = rows // CHUNK

    @pl.when(j == 0)
    def _():
        values = bytes_ref[...].astype(F32)
        scale = lax.rsqrt(jnp.mean(values * values, -1, keepdims=True) + epsilon)
        normed = (values * scale * gain_ref[...]).astype(BF)
        normed_ref[...] = normed
        bc = dot(normed, wbc_ref[...])
        bc_ref[...] = bc.astype(BF)
        raw = dot(normed, wdt_ref[...]) + bias_ref[...]
        dt = jnp.maximum(raw, 0.0) + jnp.log1p(jnp.exp(-jnp.abs(raw)))
        step = dt * rate_ref[...]
        row = lax.broadcasted_iota(jnp.int32, (CHUNK, CHUNK), 0)
        col = lax.broadcasted_iota(jnp.int32, (CHUNK, CHUNK), 1)
        lower = (row >= col).astype(F32)
        log_dt = jnp.log(dt) * LOG2E
        running = jnp.zeros((1, LANES), F32)
        totals = []
        for c in range(chunks):
            at = pl.ds(c * CHUNK, CHUNK)
            part = slice(c * CHUNK, (c + 1) * CHUNK)
            cum = jnp.dot(lower, step[part], precision=highest, preferred_element_type=F32)
            cum_ref[at, :] = cum
            late = cum - log_dt[part]
            turned = late.T
            for quad in range(HEAD_COUNT // 4):
                late_ref[quad, 0:4, at] = turned[4 * quad : 4 * quad + 4]
            end = cum[CHUNK - 1 :, :]
            weight_ref[at, :] = jnp.exp2(end - cum) * dt[part]
            bt_ref[c] = bc[part, :STATE].astype(BF).astype(F32).T.astype(BF)
            totals.append(end)
            running = running + end
        for c in range(chunks):
            total_ref[c : c + 1, :] = jnp.exp2(totals[c])
        total_ref[chunks : chunks + 1, :] = jnp.exp2(running)

    x = silu(dot(normed_ref[...], wx_ref[...]))
    x_ref[...] = x.astype(BF)
    weight = quad_columns(weight_ref[...], j)
    factor = quad_columns(total_ref[...], j)
    group = send_ref.shape[0] // 2
    piece = send_ref.shape[1] - EXTRA
    for pair in range(2):
        lanes = slice(pair * LANES, (pair + 1) * LANES)
        spread = pair_lanes(weight, pair)
        decay = pair_lanes(factor, pair)
        decay_ref[:, lanes] = decay
        scaled = (x[:, lanes] * spread).astype(BF)
        state = None
        for c in range(chunks):
            part = slice(c * CHUNK, (c + 1) * CHUNK)
            local = dot(bt_ref[c], scaled[part])
            local_ref[c, pair] = local.astype(BF)
            state = local if c == 0 else state * decay[c : c + 1] + local
        whole_decay = decay[chunks : chunks + 1]
        high = whole_decay.astype(BF).astype(F32)
        low = whole_decay - high
        row = lax.broadcasted_iota(jnp.int32, (EXTRA, LANES), 0)
        tail = jnp.where(row == 0, high, jnp.where(row == 1, low, 0.0)).astype(BF)
        for d in range(group):
            send_ref[pair * group + d, :piece, :] = state[d * piece : (d + 1) * piece].astype(BF)
            send_ref[pair * group + d, piece:, :] = tail


def scan_states(byte_states, gain, mamba_in, mamba_bc, mamba_dt, bias, rate, devices):
    rows, width = byte_states.shape
    chunks = rows // CHUNK
    steps = INNER_WIDTH // QUAD
    piece = INNER_WIDTH * STATE // (LANES * devices)
    pairs = HEAD_COUNT // 2
    return pl.pallas_call(
        states_body,
        grid=(steps,),
        in_specs=[
            whole((rows, width)),
            whole((1, width)),
            pl.BlockSpec((width, QUAD), lambda j: (0, j)),
            whole((width, 2 * STATE)),
            whole((width, LANES)),
            whole((1, LANES)),
            whole((1, LANES)),
        ],
        out_specs=[
            whole((rows, width)),
            pl.BlockSpec((rows, QUAD), lambda j: (0, j)),
            whole((rows, 2 * STATE)),
            whole((rows, LANES)),
            whole((steps, 8, rows)),
            pl.BlockSpec((chunks, 2, STATE, LANES), lambda j: (0, j, 0, 0)),
            pl.BlockSpec((8, QUAD), lambda j: (0, j)),
            pl.BlockSpec((devices // steps, piece + EXTRA, LANES), lambda j: (j, 0, 0)),
        ],
        out_shape=[
            jax.ShapeDtypeStruct((rows, width), BF),
            jax.ShapeDtypeStruct((rows, INNER_WIDTH), BF),
            jax.ShapeDtypeStruct((rows, 2 * STATE), BF),
            jax.ShapeDtypeStruct((rows, LANES), F32),
            jax.ShapeDtypeStruct((steps, 8, rows), F32),
            jax.ShapeDtypeStruct((chunks, pairs, STATE, LANES), BF),
            jax.ShapeDtypeStruct((8, INNER_WIDTH), F32),
            jax.ShapeDtypeStruct((devices, piece + EXTRA, LANES), BF),
        ],
        scratch_shapes=[
            pltpu.VMEM((chunks, STATE, CHUNK), BF),
            pltpu.VMEM((rows, LANES), F32),
            pltpu.VMEM((8, LANES), F32),
        ],
        compiler_params=params(),
        name="scan_states",
    )(byte_states, gain, mamba_in, mamba_bc, mamba_dt, bias, rate)


def prefix_body(parts_ref, out_ref):
    devices, piece, _ = out_ref.shape
    state = jnp.zeros((piece, LANES), F32)
    for d in range(devices):
        out_ref[d] = state.astype(BF)
        tail = parts_ref[d, piece:, :].astype(F32)
        decay = tail[0:1] + tail[1:2]
        state = state * decay + parts_ref[d, :piece, :].astype(F32)


def state_prefix(parts):
    devices, rows, _ = parts.shape
    piece = rows - EXTRA
    return pl.pallas_call(
        prefix_body,
        grid=(1,),
        in_specs=[whole(parts.shape)],
        out_specs=whole((devices, piece, LANES)),
        out_shape=jax.ShapeDtypeStruct((devices, piece, LANES), BF),
        compiler_params=params(),
        name="state_prefix",
    )(parts)


def within_body(
    normed_ref, wg_ref, x_ref, bc_ref, cum_ref, late_ref, skip_ref, y_ref, gate_ref, contact_ref
):
    j = pl.program_id(0)
    rows = normed_ref.shape[0]
    chunks = rows // CHUNK

    @pl.when(j == 0)
    def _():
        row = lax.broadcasted_iota(jnp.int32, (CHUNK, CHUNK), 0)
        col = lax.broadcasted_iota(jnp.int32, (CHUNK, CHUNK), 1)
        for c in range(chunks):
            at = pl.ds(c * CHUNK, CHUNK)
            contact = dot_t(bc_ref[at, STATE:], bc_ref[at, :STATE])
            contact_ref[c] = jnp.where(row >= col, contact, 0.0)

    gate_ref[...] = silu(dot(normed_ref[...], wg_ref[...])).astype(BF)
    cum = quad_columns(cum_ref[...], j)
    lane = lax.broadcasted_iota(jnp.int32, (CHUNK, LANES), 1)
    for c in range(chunks):
        at = pl.ds(c * CHUNK, CHUNK)
        part = slice(c * CHUNK, (c + 1) * CHUNK)
        for pair in range(2):
            lanes = slice(pair * LANES, (pair + 1) * LANES)
            weights = []
            for head in (2 * pair, 2 * pair + 1):
                late = late_ref[0, head : head + 1, at]
                gap = cum[part, head : head + 1] - late
                weights.append((jnp.exp2(jnp.minimum(gap, 126.0)) * contact_ref[c]).astype(BF))
            x = x_ref[at, lanes]
            zero = jnp.zeros_like(x)
            stacked = jnp.concatenate(
                [jnp.where(lane < HEAD_WIDTH, x, zero), jnp.where(lane < HEAD_WIDTH, zero, x)], 0
            )
            inner = dot(jnp.concatenate(weights, 1), stacked)
            y_ref[at, lanes] = inner + skip_ref[:, lanes] * x.astype(F32)


def scan_within(normed, mamba_in, x, bc, cum, late, skip):
    rows, width = normed.shape
    chunks = rows // CHUNK
    steps = INNER_WIDTH // QUAD
    return pl.pallas_call(
        within_body,
        grid=(steps,),
        in_specs=[
            whole((rows, width)),
            pl.BlockSpec((width, QUAD), lambda j: (0, j + steps)),
            pl.BlockSpec((rows, QUAD), lambda j: (0, j)),
            whole((rows, 2 * STATE)),
            whole((rows, LANES)),
            pl.BlockSpec((1, 8, rows), lambda j: (j, 0, 0)),
            pl.BlockSpec((1, QUAD), lambda j: (0, j)),
        ],
        out_specs=[
            pl.BlockSpec((rows, QUAD), lambda j: (0, j)),
            pl.BlockSpec((rows, QUAD), lambda j: (0, j)),
        ],
        out_shape=[
            jax.ShapeDtypeStruct((rows, INNER_WIDTH), F32),
            jax.ShapeDtypeStruct((rows, INNER_WIDTH), BF),
        ],
        scratch_shapes=[pltpu.VMEM((chunks, CHUNK, CHUNK), F32)],
        compiler_params=params(),
        name="scan_within",
    )(normed, mamba_in, x, bc, cum, late, skip)


def finish_body(
    y_ref, gate_ref, bc_ref, cum_ref, incoming_ref, local_ref, decay_ref, gain_ref, wo_ref,
    bytes_ref, rank_ref, encoded_ref, spans_ref, acc_ref, square_ref,
):
    j = pl.program_id(0)
    rows = y_ref.shape[0]
    chunks = rows // CHUNK

    @pl.when(j == 0)
    def _():
        acc_ref[...] = jnp.zeros_like(acc_ref)
        square_ref[...] = jnp.zeros_like(square_ref)

    grown = quad_columns(jnp.exp2(cum_ref[...]), j)
    columns = []
    for pair in range(2):
        lanes = slice(pair * LANES, (pair + 1) * LANES)
        spread = pair_lanes(grown, pair)
        state = incoming_ref[pair].astype(F32)
        pieces = []
        for c in range(chunks):
            at = pl.ds(c * CHUNK, CHUNK)
            part = slice(c * CHUNK, (c + 1) * CHUNK)
            carried = dot(bc_ref[at, STATE:], state.astype(BF))
            gated = (y_ref[at, lanes] + carried * spread[part]) * gate_ref[at, lanes].astype(F32)
            square_ref[at, :] += gated * gated
            pieces.append((gated * gain_ref[:, lanes]).astype(BF))
            state = state * decay_ref[c : c + 1, lanes] + local_ref[c, pair].astype(F32)
        columns.append(jnp.concatenate(pieces, 0))
    acc_ref[...] += dot(jnp.concatenate(columns, 1), wo_ref[...])

    @pl.when(j == pl.num_programs(0) - 1)
    def _():
        mean = jnp.sum(square_ref[...], -1, keepdims=True) * (1.0 / INNER_WIDTH)
        mixed = acc_ref[...] * lax.rsqrt(mean + epsilon)
        encoded = (bytes_ref[...].astype(F32) + mixed).astype(BF)
        encoded_ref[...] = encoded
        slot = lax.broadcasted_iota(jnp.int32, (CAP, rows), 0)
        picker = jnp.where(rank_ref[...] == slot, 1.0, 0.0).astype(BF)
        spans_ref[...] = dot(picker, encoded).astype(BF)


def scan_finish(y, gate, bc, cum, incoming, local, decay, gain, mamba_out, byte_states, rank):
    rows, width = byte_states.shape
    chunks = rows // CHUNK
    steps = INNER_WIDTH // QUAD
    return pl.pallas_call(
        finish_body,
        grid=(steps,),
        in_specs=[
            pl.BlockSpec((rows, QUAD), lambda j: (0, j)),
            pl.BlockSpec((rows, QUAD), lambda j: (0, j)),
            whole((rows, 2 * STATE)),
            whole((rows, LANES)),
            pl.BlockSpec((2, STATE, LANES), lambda j: (j, 0, 0)),
            pl.BlockSpec((chunks, 2, STATE, LANES), lambda j: (0, j, 0, 0)),
            pl.BlockSpec((8, QUAD), lambda j: (0, j)),
            pl.BlockSpec((1, QUAD), lambda j: (0, j)),
            pl.BlockSpec((QUAD, width), lambda j: (j, 0)),
            whole((rows, width)),
            whole((1, rows)),
        ],
        out_specs=[whole((rows, width)), whole((CAP, width))],
        out_shape=[
            jax.ShapeDtypeStruct((rows, width), BF),
            jax.ShapeDtypeStruct((CAP, width), BF),
        ],
        scratch_shapes=[pltpu.VMEM((rows, width), F32), pltpu.VMEM((rows, LANES), F32)],
        compiler_params=params(),
        name="scan_finish",
    )(y, gate, bc, cum, incoming, local, decay, gain, mamba_out, byte_states, rank)


def attention_body(
    index_ref, q_ref, kv_ref, bias_ref, out_ref, top_ref, total_ref, acc_ref, *, heads, block
):
    piece = pl.program_id(0)
    mine = index_ref[0]
    source = index_ref[1 + piece]
    slots = q_ref.shape[0]

    @pl.when(piece == 0)
    def _():
        top_ref[...] = jnp.full_like(top_ref, -1e30)
        total_ref[...] = jnp.zeros_like(total_ref)
        acc_ref[...] = jnp.zeros_like(acc_ref)

    def attend(diagonal):
        for h in range(heads):
            keys = slice(h * 2 * HD, h * 2 * HD + HD)
            vals = slice(h * 2 * HD + HD, (h + 1) * 2 * HD)
            for b in range(slots // block):
                at = pl.ds(b * block, block)
                span = (b + 1) * block if diagonal else slots
                scores = dot_t(q_ref[at, h * HD : (h + 1) * HD], kv_ref[0, :span, keys])
                scores = scores + bias_ref[0, :, :span]
                if diagonal:
                    row = lax.broadcasted_iota(jnp.int32, scores.shape, 0) + b * block
                    col = lax.broadcasted_iota(jnp.int32, scores.shape, 1)
                    scores = jnp.where(col <= row, scores, -2e30)
                old = top_ref[h, at, :]
                top = jnp.maximum(old, jnp.max(scores, -1, keepdims=True))
                rescale = jnp.exp2(old - top)
                numer = jnp.exp2(scores - top[:, :1])
                top_ref[h, at, :] = top
                total_ref[h, at, :] = total_ref[h, at, :] * rescale + jnp.sum(
                    numer, -1, keepdims=True
                )
                acc_ref[h, at, :] = acc_ref[h, at, :] * rescale + dot(
                    numer.astype(BF), kv_ref[0, :span, vals]
                )

    @pl.when(source == mine)
    def _():
        attend(True)

    @pl.when(source < mine)
    def _():
        attend(False)

    @pl.when(piece == pl.num_programs(0) - 1)
    def _():
        for h in range(heads):
            out_ref[:, h * HD : (h + 1) * HD] = (acc_ref[h] / total_ref[h]).astype(BF)


def attention(index, q, kv, bias, heads):
    pieces, slots, width = kv.shape
    return pl.pallas_call(
        functools.partial(attention_body, heads=heads, block=256),
        grid_spec=pltpu.PrefetchScalarGridSpec(
            num_scalar_prefetch=1,
            grid=(pieces,),
            in_specs=[
                pl.BlockSpec((slots, heads * HD), lambda p, i: (0, 0)),
                pl.BlockSpec((1, slots, width), lambda p, i: (p, 0, 0)),
                pl.BlockSpec((1, 1, slots), lambda p, i: (p, 0, 0)),
            ],
            out_specs=pl.BlockSpec((slots, heads * HD), lambda p, i: (0, 0)),
            scratch_shapes=[pltpu.VMEM((heads, slots, HD), F32)] * 3,
        ),
        out_shape=jax.ShapeDtypeStruct((slots, heads * HD), BF),
        compiler_params=params(),
        name="attention",
    )(index, q, kv, bias)


def earlier_shards(kv, axis):
    count = lax.axis_size(axis)
    partner = [(i, i ^ 1) for i in range(count)]
    got = [lax.ppermute(kv, axis, partner)]
    for k in range(2, count, 2):
        direct = lax.ppermute(kv, axis, [(i - k, i) for i in range(k, count)])
        got.append(direct)
        got.append(lax.ppermute(direct, axis, partner))
    return got


def local(
    byte_states,
    boundary_flags,
    span_counts,
    enc_norm_gain,
    mamba_in,
    mamba_bc,
    mamba_dt,
    dt_bias,
    decay_rate,
    skip_gain,
    gate_norm_gain,
    mamba_out,
    down_proj,
    attn_norm_gain,
    qkv_weight,
    out_weight,
    up_proj,
):
    axes = ("main", "sub")
    devices = lax.axis_size(axes)
    subs = lax.axis_size("sub")
    mains = lax.axis_size("main")
    main_id = lax.axis_index("main")
    rows, width = byte_states.shape
    heads = qkv_weight.shape[1]
    model = qkv_weight.shape[0]

    pad = ((0, 0), (0, LANES - HEAD_COUNT))
    normed, x, bc, cum, late, chunk_states, decay, send = scan_states(
        byte_states,
        enc_norm_gain[None],
        mamba_in,
        mamba_bc,
        jnp.pad(mamba_dt, pad),
        jnp.pad(dt_bias[None], pad),
        jnp.pad(-LOG2E * decay_rate[None], pad),
        devices,
    )
    parts = lax.all_to_all(send, axes, 0, 0, tiled=True)
    y, gate = scan_within(
        normed, mamba_in, x, bc, cum, late, jnp.repeat(skip_gain, HEAD_WIDTH)[None]
    )
    incoming = lax.all_to_all(state_prefix(parts), axes, 0, 0, tiled=True)
    incoming = incoming.reshape(HEAD_COUNT // 2, STATE, LANES)

    scaled_qkv = (attn_norm_gain[:, None] * qkv_weight.reshape(model, -1).astype(F32)).astype(BF)
    down_qkv = dot(down_proj, scaled_qkv).astype(BF)
    out_up = dot(out_weight.reshape(heads * HD, model), up_proj).astype(BF)
    out_up_all = lax.all_gather(out_up, "sub", axis=0, tiled=True)

    span_rank = jnp.cumsum(boundary_flags) - 1
    picked = jnp.where(boundary_flags == 1, span_rank, -1)
    encoded, span_rows = scan_finish(
        y,
        gate,
        bc,
        cum,
        incoming,
        chunk_states,
        decay,
        gate_norm_gain[None],
        mamba_out,
        byte_states,
        picked[None],
    )

    main_in = dot(span_rows, down_proj).astype(BF)
    wide = main_in.astype(F32)
    scale = lax.rsqrt(jnp.mean(wide * wide, -1, keepdims=True) + epsilon)
    sent_rows = (span_rows.astype(F32) * scale).astype(BF)
    shard_rows = lax.all_to_all(
        jnp.broadcast_to(sent_rows[None], (subs, CAP, width)), "sub", 0, 0
    ).reshape(subs * CAP, width)
    qkv = dot(shard_rows, down_qkv)
    slots = qkv.shape[0]
    qkv = qkv.reshape(slots, heads, 3 * HD)
    queries = (qkv[:, :, :HD].reshape(slots, heads * HD) * (HD**-0.5 * LOG2E)).astype(BF)
    kv = qkv[:, :, HD:].reshape(slots, heads * 2 * HD).astype(BF)
    shards = [kv] + earlier_shards(kv, "main")
    sources = [main_id, main_id ^ 1]
    for k in range(2, mains, 2):
        sources += [main_id - k, (main_id ^ 1) - k]
    sources = [jnp.where(s < 0, mains, s) for s in sources]
    slot = jnp.arange(slots, dtype=jnp.int32)
    valid = slot[None] % CAP < jnp.repeat(
        span_counts.reshape(mains, subs), CAP, axis=1
    )
    bias = jnp.where(valid, 0.0, -1e30).astype(F32)
    index = jnp.stack([main_id] + sources).astype(jnp.int32)
    bias = jnp.take(bias, jnp.minimum(index[1:], mains - 1), axis=0)[:, None, :]
    heads_out = attention(index, queries, jnp.stack(shards), bias, heads)
    own_heads = lax.all_to_all(heads_out.reshape(subs, CAP, heads * HD), "sub", 0, 0)
    flat_heads = own_heads.transpose(1, 0, 2).reshape(CAP, subs * heads * HD)
    span_up = (dot(main_in, up_proj) + dot(flat_heads, out_up_all)).astype(BF)

    device_ids = jnp.arange(span_counts.shape[0], dtype=jnp.int32)
    slot_ids = jnp.arange(CAP, dtype=jnp.int32)
    device_id = main_id * subs + lax.axis_index("sub")
    own_count = jnp.sum(jnp.where(device_ids == device_id, span_counts, 0))
    edge_slots = own_count - jnp.array([2, 1], jnp.int32)
    edge_pick = (slot_ids[None, :] == edge_slots[:, None]).astype(BF)
    edge_rows = dot(edge_pick, span_up).astype(BF)
    previous = lax.ppermute(edge_rows, axes, [(i, i + 1) for i in range(devices - 1)])
    table = jnp.concatenate([previous, span_up], 0)
    target = span_rank + 1
    spread = (target[:, None] == jnp.arange(CAP + 2)[None, :]).astype(BF)
    return (encoded.astype(F32) + dot(spread, table)).astype(BF)


def solution(mesh):
    return jax.shard_map(
        local,
        mesh=mesh,
        in_specs=(
            P(("main", "sub"), None),
            P(("main", "sub")),
            P(),
            P(),
            P(),
            P(),
            P(),
            P(),
            P(),
            P(),
            P(),
            P(),
            P(),
            P(),
            P(None, "sub", None),
            P("sub", None, None),
            P(),
        ),
        out_specs=P(("main", "sub"), None),
        check_vma=False,
    )
```

```python
import functools
import math

import jax
import jax.numpy as jnp
from jax import lax
from jax.experimental import pallas as pl
from jax.experimental.pallas import tpu as pltpu
from jax.sharding import PartitionSpec as P

INNER_WIDTH = 2048
HEAD_COUNT = 32
HEAD_WIDTH = 64
STATE = 128
HD = 128
CAP = 96
CHUNK = 128
LANES = 128
QUAD = 256
EXTRA = 16

epsilon = 1e-06
highest = lax.Precision.HIGHEST
LOG2E = math.log2(math.e)
BF = jnp.bfloat16
F32 = jnp.float32


def dot(a, b, **kw):
    return jnp.dot(a, b, preferred_element_type=F32, **kw)


def dot_t(a, b):
    return lax.dot_general(a, b, (((1,), (1,)), ((), ())), preferred_element_type=F32)


def silu(v):
    return v * jax.nn.sigmoid(v)


def params(**kw):
    return pltpu.CompilerParams(dimension_semantics=("arbitrary",), **kw)


def whole(shape):
    rank = len(shape)
    return pl.BlockSpec(shape, lambda j: (0,) * rank)


def pair_lanes(columns, pair):
    rows = columns.shape[0]
    low = jnp.broadcast_to(columns[:, 2 * pair : 2 * pair + 1], (rows, LANES))
    high = jnp.broadcast_to(columns[:, 2 * pair + 1 : 2 * pair + 2], (rows, LANES))
    lane = lax.broadcasted_iota(jnp.int32, (rows, LANES), 1)
    return jnp.where(lane < HEAD_WIDTH, low, high)


def padded(row_ref):
    return jnp.concatenate([row_ref[...], jnp.zeros((1, LANES - HEAD_COUNT), F32)], 1)


def quad_columns(table, j):
    return pltpu.roll(table, (LANES - 4 * j) % LANES, 1)


def states_body(
    bytes_ref, gain_ref, wx_ref, wbc_ref, wdt_ref, bias_ref, rate_ref,
    normed_ref, x_ref, bc_ref, cum_ref, late_ref, local_ref, decay_ref, send_ref,
    bt_ref, weight_ref, total_ref,
):
    j = pl.program_id(0)
    rows = bytes_ref.shape[0]
    chunks = rows // CHUNK

    @pl.when(j == 0)
    def _():
        values = bytes_ref[...].astype(F32)
        scale = lax.rsqrt(jnp.mean(values * values, -1, keepdims=True) + epsilon)
        normed = (values * scale * gain_ref[...]).astype(BF)
        normed_ref[...] = normed
        bc = dot(normed, wbc_ref[...])
        bc_ref[...] = bc.astype(BF)
        spare = jnp.zeros((LANES - HEAD_COUNT, normed.shape[1]), BF)
        raw = dot_t(normed, jnp.concatenate([wdt_ref[...], spare], 0)) + padded(bias_ref)
        dt = jnp.maximum(raw, 0.0) + jnp.log1p(jnp.exp(-jnp.abs(raw)))
        step = dt * (-LOG2E * padded(rate_ref))
        row = lax.broadcasted_iota(jnp.int32, (CHUNK, CHUNK), 0)
        col = lax.broadcasted_iota(jnp.int32, (CHUNK, CHUNK), 1)
        lower = (row >= col).astype(F32)
        log_dt = jnp.log(dt) * LOG2E
        running = jnp.zeros((1, LANES), F32)
        totals = []
        for c in range(chunks):
            at = pl.ds(c * CHUNK, CHUNK)
            part = slice(c * CHUNK, (c + 1) * CHUNK)
            cum = jnp.dot(lower, step[part], precision=highest, preferred_element_type=F32)
            cum_ref[at, :] = cum
            late = cum - log_dt[part]
            turned = late.T
            for quad in range(HEAD_COUNT // 4):
                late_ref[quad, 0:4, at] = turned[4 * quad : 4 * quad + 4]
            end = cum[CHUNK - 1 :, :]
            weight_ref[at, :] = jnp.exp2(end - cum) * dt[part]
            bt_ref[c] = bc[part, :STATE].astype(BF).astype(F32).T.astype(BF)
            totals.append(end)
            running = running + end
        for c in range(chunks):
            total_ref[c : c + 1, :] = jnp.exp2(totals[c])
        total_ref[chunks : chunks + 1, :] = jnp.exp2(running)

    x = silu(dot(normed_ref[...], wx_ref[...]))
    x_ref[...] = x.astype(BF)
    weight = quad_columns(weight_ref[...], j)
    factor = quad_columns(total_ref[...], j)
    group = send_ref.shape[0] // 2
    piece = send_ref.shape[1] - EXTRA
    for pair in range(2):
        lanes = slice(pair * LANES, (pair + 1) * LANES)
        spread = pair_lanes(weight, pair)
        decay = pair_lanes(factor, pair)
        decay_ref[:, lanes] = decay
        scaled = (x[:, lanes] * spread).astype(BF)
        state = None
        for c in range(chunks):
            part = slice(c * CHUNK, (c + 1) * CHUNK)
            local = dot(bt_ref[c], scaled[part])
            local_ref[c, pair] = local.astype(BF)
            state = local if c == 0 else state * decay[c : c + 1] + local
        whole_decay = decay[chunks : chunks + 1]
        high = whole_decay.astype(BF).astype(F32)
        low = whole_decay - high
        row = lax.broadcasted_iota(jnp.int32, (EXTRA, LANES), 0)
        tail = jnp.where(row == 0, high, jnp.where(row == 1, low, 0.0)).astype(BF)
        for d in range(group):
            send_ref[pair * group + d, :piece, :] = state[d * piece : (d + 1) * piece].astype(BF)
            send_ref[pair * group + d, piece:, :] = tail


def scan_states(byte_states, gain, mamba_in, mamba_bc, mamba_dt, bias, rate, devices):
    rows, width = byte_states.shape
    chunks = rows // CHUNK
    steps = INNER_WIDTH // QUAD
    piece = INNER_WIDTH * STATE // (LANES * devices)
    pairs = HEAD_COUNT // 2
    return pl.pallas_call(
        states_body,
        grid=(steps,),
        in_specs=[
            whole((rows, width)),
            whole((1, width)),
            pl.BlockSpec((width, QUAD), lambda j: (0, j)),
            whole((width, 2 * STATE)),
            whole((HEAD_COUNT, width)),
            whole((1, HEAD_COUNT)),
            whole((1, HEAD_COUNT)),
        ],
        out_specs=[
            whole((rows, width)),
            pl.BlockSpec((rows, QUAD), lambda j: (0, j)),
            whole((rows, 2 * STATE)),
            whole((rows, LANES)),
            whole((steps, 8, rows)),
            pl.BlockSpec((chunks, 2, STATE, LANES), lambda j: (0, j, 0, 0)),
            pl.BlockSpec((8, QUAD), lambda j: (0, j)),
            pl.BlockSpec((devices // steps, piece + EXTRA, LANES), lambda j: (j, 0, 0)),
        ],
        out_shape=[
            jax.ShapeDtypeStruct((rows, width), BF),
            jax.ShapeDtypeStruct((rows, INNER_WIDTH), BF),
            jax.ShapeDtypeStruct((rows, 2 * STATE), BF),
            jax.ShapeDtypeStruct((rows, LANES), F32),
            jax.ShapeDtypeStruct((steps, 8, rows), F32),
            jax.ShapeDtypeStruct((chunks, pairs, STATE, LANES), BF),
            jax.ShapeDtypeStruct((8, INNER_WIDTH), F32),
            jax.ShapeDtypeStruct((devices, piece + EXTRA, LANES), BF),
        ],
        scratch_shapes=[
            pltpu.VMEM((chunks, STATE, CHUNK), BF),
            pltpu.VMEM((rows, LANES), F32),
            pltpu.VMEM((8, LANES), F32),
        ],
        compiler_params=params(),
        name="scan_states",
    )(byte_states, gain, mamba_in, mamba_bc, mamba_dt, bias, rate)


def prefix_body(parts_ref, out_ref):
    devices, piece, _ = out_ref.shape
    state = jnp.zeros((piece, LANES), F32)
    for d in range(devices):
        out_ref[d] = state.astype(BF)
        tail = parts_ref[d, piece:, :].astype(F32)
        decay = tail[0:1] + tail[1:2]
        state = state * decay + parts_ref[d, :piece, :].astype(F32)


def state_prefix(parts):
    devices, rows, _ = parts.shape
    piece = rows - EXTRA
    return pl.pallas_call(
        prefix_body,
        grid=(1,),
        in_specs=[whole(parts.shape)],
        out_specs=whole((devices, piece, LANES)),
        out_shape=jax.ShapeDtypeStruct((devices, piece, LANES), BF),
        compiler_params=params(),
        name="state_prefix",
    )(parts)


def within_body(
    normed_ref, wg_ref, x_ref, bc_ref, cum_ref, late_ref, skip_ref, y_ref, gate_ref, contact_ref
):
    j = pl.program_id(0)
    rows = normed_ref.shape[0]
    chunks = rows // CHUNK

    @pl.when(j == 0)
    def _():
        row = lax.broadcasted_iota(jnp.int32, (CHUNK, CHUNK), 0)
        col = lax.broadcasted_iota(jnp.int32, (CHUNK, CHUNK), 1)
        for c in range(chunks):
            at = pl.ds(c * CHUNK, CHUNK)
            contact = dot_t(bc_ref[at, STATE:], bc_ref[at, :STATE])
            contact_ref[c] = jnp.where(row >= col, contact, 0.0)

    gate_ref[...] = silu(dot(normed_ref[...], wg_ref[...])).astype(BF)
    cum = quad_columns(cum_ref[...], j)
    skip = quad_columns(jnp.broadcast_to(padded(skip_ref), (8, LANES)), j)
    skips = [pair_lanes(skip, pair)[:1] for pair in range(2)]
    lane = lax.broadcasted_iota(jnp.int32, (CHUNK, LANES), 1)
    for c in range(chunks):
        at = pl.ds(c * CHUNK, CHUNK)
        part = slice(c * CHUNK, (c + 1) * CHUNK)
        for pair in range(2):
            lanes = slice(pair * LANES, (pair + 1) * LANES)
            weights = []
            for head in (2 * pair, 2 * pair + 1):
                late = late_ref[0, head : head + 1, at]
                gap = cum[part, head : head + 1] - late
                weights.append((jnp.exp2(jnp.minimum(gap, 126.0)) * contact_ref[c]).astype(BF))
            x = x_ref[at, lanes]
            zero = jnp.zeros_like(x)
            stacked = jnp.concatenate(
                [jnp.where(lane < HEAD_WIDTH, x, zero), jnp.where(lane < HEAD_WIDTH, zero, x)], 0
            )
            inner = dot(jnp.concatenate(weights, 1), stacked)
            y_ref[at, lanes] = inner + skips[pair] * x.astype(F32)


def scan_within(normed, mamba_in, x, bc, cum, late, skip):
    rows, width = normed.shape
    chunks = rows // CHUNK
    steps = INNER_WIDTH // QUAD
    return pl.pallas_call(
        within_body,
        grid=(steps,),
        in_specs=[
            whole((rows, width)),
            pl.BlockSpec((width, QUAD), lambda j: (0, j + steps)),
            pl.BlockSpec((rows, QUAD), lambda j: (0, j)),
            whole((rows, 2 * STATE)),
            whole((rows, LANES)),
            pl.BlockSpec((1, 8, rows), lambda j: (j, 0, 0)),
            whole((1, HEAD_COUNT)),
        ],
        out_specs=[
            pl.BlockSpec((rows, QUAD), lambda j: (0, j)),
            pl.BlockSpec((rows, QUAD), lambda j: (0, j)),
        ],
        out_shape=[
            jax.ShapeDtypeStruct((rows, INNER_WIDTH), F32),
            jax.ShapeDtypeStruct((rows, INNER_WIDTH), BF),
        ],
        scratch_shapes=[pltpu.VMEM((chunks, CHUNK, CHUNK), F32)],
        compiler_params=params(),
        name="scan_within",
    )(normed, mamba_in, x, bc, cum, late, skip)


def finish_body(
    y_ref, gate_ref, bc_ref, cum_ref, incoming_ref, local_ref, decay_ref, gain_ref, wo_ref,
    bytes_ref, rank_ref, encoded_ref, spans_ref, acc_ref, square_ref,
):
    j = pl.program_id(0)
    rows = y_ref.shape[0]
    chunks = rows // CHUNK

    @pl.when(j == 0)
    def _():
        acc_ref[...] = jnp.zeros_like(acc_ref)
        square_ref[...] = jnp.zeros_like(square_ref)

    grown = quad_columns(jnp.exp2(cum_ref[...]), j)
    columns = []
    for pair in range(2):
        lanes = slice(pair * LANES, (pair + 1) * LANES)
        spread = pair_lanes(grown, pair)
        state = incoming_ref[pair].astype(F32)
        pieces = []
        for c in range(chunks):
            at = pl.ds(c * CHUNK, CHUNK)
            part = slice(c * CHUNK, (c + 1) * CHUNK)
            carried = dot(bc_ref[at, STATE:], state.astype(BF))
            gated = (y_ref[at, lanes] + carried * spread[part]) * gate_ref[at, lanes].astype(F32)
            square_ref[at, :] += gated * gated
            pieces.append((gated * gain_ref[:, lanes]).astype(BF))
            state = state * decay_ref[c : c + 1, lanes] + local_ref[c, pair].astype(F32)
        columns.append(jnp.concatenate(pieces, 0))
    acc_ref[...] += dot(jnp.concatenate(columns, 1), wo_ref[...])

    @pl.when(j == pl.num_programs(0) - 1)
    def _():
        mean = jnp.sum(square_ref[...], -1, keepdims=True) * (1.0 / INNER_WIDTH)
        mixed = acc_ref[...] * lax.rsqrt(mean + epsilon)
        encoded = (bytes_ref[...].astype(F32) + mixed).astype(BF)
        encoded_ref[...] = encoded
        slot = lax.broadcasted_iota(jnp.int32, (CAP, rows), 0)
        picker = jnp.where(rank_ref[...] == slot, 1.0, 0.0).astype(BF)
        spans_ref[...] = dot(picker, encoded).astype(BF)


def scan_finish(y, gate, bc, cum, incoming, local, decay, gain, mamba_out, byte_states, rank):
    rows, width = byte_states.shape
    chunks = rows // CHUNK
    steps = INNER_WIDTH // QUAD
    return pl.pallas_call(
        finish_body,
        grid=(steps,),
        in_specs=[
            pl.BlockSpec((rows, QUAD), lambda j: (0, j)),
            pl.BlockSpec((rows, QUAD), lambda j: (0, j)),
            whole((rows, 2 * STATE)),
            whole((rows, LANES)),
            pl.BlockSpec((2, STATE, LANES), lambda j: (j, 0, 0)),
            pl.BlockSpec((chunks, 2, STATE, LANES), lambda j: (0, j, 0, 0)),
            pl.BlockSpec((8, QUAD), lambda j: (0, j)),
            pl.BlockSpec((1, QUAD), lambda j: (0, j)),
            pl.BlockSpec((QUAD, width), lambda j: (j, 0)),
            whole((rows, width)),
            whole((1, rows)),
        ],
        out_specs=[whole((rows, width)), whole((CAP, width))],
        out_shape=[
            jax.ShapeDtypeStruct((rows, width), BF),
            jax.ShapeDtypeStruct((CAP, width), BF),
        ],
        scratch_shapes=[pltpu.VMEM((rows, width), F32), pltpu.VMEM((rows, LANES), F32)],
        compiler_params=params(),
        name="scan_finish",
    )(y, gate, bc, cum, incoming, local, decay, gain, mamba_out, byte_states, rank)


def attention_body(
    index_ref, q_ref, kv_ref, bias_ref, out_ref, top_ref, total_ref, acc_ref, *, heads, block
):
    piece = pl.program_id(0)
    mine = index_ref[0]
    source = index_ref[1 + piece]
    slots = q_ref.shape[0]

    @pl.when(piece == 0)
    def _():
        top_ref[...] = jnp.full_like(top_ref, -1e30)
        total_ref[...] = jnp.zeros_like(total_ref)
        acc_ref[...] = jnp.zeros_like(acc_ref)

    def attend(diagonal):
        for h in range(heads):
            keys = slice(h * 2 * HD, h * 2 * HD + HD)
            vals = slice(h * 2 * HD + HD, (h + 1) * 2 * HD)
            for b in range(slots // block):
                at = pl.ds(b * block, block)
                span = (b + 1) * block if diagonal else slots
                scores = dot_t(q_ref[at, h * HD : (h + 1) * HD], kv_ref[0, :span, keys])
                scores = scores + bias_ref[0, :, :span]
                if diagonal:
                    row = lax.broadcasted_iota(jnp.int32, scores.shape, 0) + b * block
                    col = lax.broadcasted_iota(jnp.int32, scores.shape, 1)
                    scores = jnp.where(col <= row, scores, -2e30)
                old = top_ref[h, at, :]
                top = jnp.maximum(old, jnp.max(scores, -1, keepdims=True))
                rescale = jnp.exp2(old - top)
                numer = jnp.exp2(scores - top[:, :1])
                top_ref[h, at, :] = top
                total_ref[h, at, :] = total_ref[h, at, :] * rescale + jnp.sum(
                    numer, -1, keepdims=True
                )
                acc_ref[h, at, :] = acc_ref[h, at, :] * rescale + dot(
                    numer.astype(BF), kv_ref[0, :span, vals]
                )

    @pl.when(source == mine)
    def _():
        attend(True)

    @pl.when(source < mine)
    def _():
        attend(False)

    @pl.when(piece == pl.num_programs(0) - 1)
    def _():
        for h in range(heads):
            out_ref[:, h * HD : (h + 1) * HD] = (acc_ref[h] / total_ref[h]).astype(BF)


def attention(index, q, kv, bias, heads):
    pieces, slots, width = kv.shape
    return pl.pallas_call(
        functools.partial(attention_body, heads=heads, block=256),
        grid_spec=pltpu.PrefetchScalarGridSpec(
            num_scalar_prefetch=1,
            grid=(pieces,),
            in_specs=[
                pl.BlockSpec((slots, heads * HD), lambda p, i: (0, 0)),
                pl.BlockSpec((1, slots, width), lambda p, i: (p, 0, 0)),
                pl.BlockSpec((1, 1, slots), lambda p, i: (p, 0, 0)),
            ],
            out_specs=pl.BlockSpec((slots, heads * HD), lambda p, i: (0, 0)),
            scratch_shapes=[pltpu.VMEM((heads, slots, HD), F32)] * 3,
        ),
        out_shape=jax.ShapeDtypeStruct((slots, heads * HD), BF),
        compiler_params=params(),
        name="attention",
    )(index, q, kv, bias)


def sub_grid(count):
    minor = 1
    while minor * minor * 4 <= count:
        minor *= 2
    return count // minor, minor


def gather_sub(block, axis):
    count = lax.axis_size(axis)
    major, minor = sub_grid(count)

    def move(value, dz, dx):
        route = []
        for i in range(count):
            z, x = divmod(i, minor)
            route.append((i, (z + dz) % major * minor + (x + dx) % minor))
        return lax.ppermute(value, axis, route)

    columns = [block] + [move(block, dz, 0) for dz in range(1, major)]
    return [columns[dz] if dx == 0 else move(columns[dz], 0, dx)
            for dz in range(major) for dx in range(minor)]


def sub_sources(axis):
    count = lax.axis_size(axis)
    major, minor = sub_grid(count)
    me = lax.axis_index(axis)
    z, x = me // minor, me % minor
    return [(z - dz) % major * minor + (x - dx) % minor
            for dz in range(major) for dx in range(minor)]


def gather_main(block, axis):
    count = lax.axis_size(axis)
    partner = [(i, i ^ 1) for i in range(count)]
    got = [block, lax.ppermute(block, axis, partner)]
    for k in range(2, count, 2):
        direct = lax.ppermute(block, axis, [(i, (i + k) % count) for i in range(count)])
        got += [direct, lax.ppermute(direct, axis, partner)]
    return got


def main_sources(axis):
    count = lax.axis_size(axis)
    me = lax.axis_index(axis)
    return [x for k in range(0, count, 2) for x in ((me - k) % count, ((me ^ 1) - k) % count)]


def qkv_body(index_ref, weight_ref, *refs):
    *pieces, q_ref, kv_ref, rows_ref = refs

    @pl.when(pl.program_id(0) == 0)
    def _():
        for p, piece in enumerate(pieces):
            rows_ref[index_ref[p]] = piece[...]

    count, cap, width = rows_ref.shape
    out = dot(rows_ref[...].reshape(count * cap, width), weight_ref[...])
    q_ref[...] = (out[:, :HD] * (HD**-0.5 * LOG2E)).astype(BF)
    kv_ref[...] = out[:, HD:].astype(BF)


def project_qkv(index, weight, pieces, heads):
    cap, width = pieces[0].shape
    slots = cap * len(pieces)
    return pl.pallas_call(
        qkv_body,
        grid_spec=pltpu.PrefetchScalarGridSpec(
            num_scalar_prefetch=1,
            grid=(heads,),
            in_specs=[pl.BlockSpec((width, 3 * HD), lambda h, i: (0, h))]
            + [pl.BlockSpec((cap, width), lambda h, i: (0, 0))] * len(pieces),
            out_specs=[
                pl.BlockSpec((slots, HD), lambda h, i: (0, h)),
                pl.BlockSpec((slots, 2 * HD), lambda h, i: (0, h)),
            ],
            scratch_shapes=[pltpu.VMEM((len(pieces), cap, width), BF)],
        ),
        out_shape=[
            jax.ShapeDtypeStruct((slots, heads * HD), BF),
            jax.ShapeDtypeStruct((slots, heads * 2 * HD), BF),
        ],
        compiler_params=params(),
        name="project_qkv",
    )(index, weight, *pieces)


def span_up_body(index_ref, main_up_ref, heads_ref, edge_ref, *refs):
    *weights, up_ref, edges_ref, columns_ref = refs
    subs, cap, inner = heads_ref.shape
    mains = len(weights)
    flat = jnp.concatenate([heads_ref[index_ref[mains + r]] for r in range(subs)], 1)
    for p, weight in enumerate(weights):
        columns_ref[index_ref[p]] = dot(flat, weight[...])
    joined = jnp.concatenate([columns_ref[p] for p in range(mains)], 1)
    up = (main_up_ref[...] + joined).astype(BF)
    up_ref[...] = up
    slot = lax.broadcasted_iota(jnp.int32, (16, cap), 1)
    row = lax.broadcasted_iota(jnp.int32, (16, cap), 0)
    picker = jnp.where((slot == edge_ref[0] - 2 + row) & (row < 2), 1.0, 0.0).astype(BF)
    edges_ref[...] = dot(picker, up).astype(BF)


def project_up(index, main_up, heads, weights, own_count):
    cap, width = main_up.shape
    subs, _, inner = heads.shape
    part = weights[0].shape[1]
    return pl.pallas_call(
        span_up_body,
        grid_spec=pltpu.PrefetchScalarGridSpec(
            num_scalar_prefetch=1,
            grid=(1,),
            in_specs=[
                pl.BlockSpec((cap, width), lambda j, i: (0, 0)),
                pl.BlockSpec((subs, cap, inner), lambda j, i: (0, 0, 0)),
                pl.BlockSpec(memory_space=pltpu.SMEM),
            ]
            + [pl.BlockSpec((subs * inner, part), lambda j, i: (0, 0))] * len(weights),
            out_specs=[
                pl.BlockSpec((cap, width), lambda j, i: (0, 0)),
                pl.BlockSpec((16, width), lambda j, i: (0, 0)),
            ],
            scratch_shapes=[pltpu.VMEM((len(weights), cap, part), F32)],
        ),
        out_shape=[
            jax.ShapeDtypeStruct((cap, width), BF),
            jax.ShapeDtypeStruct((16, width), BF),
        ],
        compiler_params=params(),
        name="project_up",
    )(index, main_up, heads, own_count, *weights)


def earlier_shards(kv, axis):
    count = lax.axis_size(axis)
    partner = [(i, i ^ 1) for i in range(count)]
    got = [lax.ppermute(kv, axis, partner)]
    for k in range(2, count, 2):
        direct = lax.ppermute(kv, axis, [(i - k, i) for i in range(k, count)])
        got.append(direct)
        got.append(lax.ppermute(direct, axis, partner))
    return got


def local(
    byte_states,
    boundary_flags,
    span_counts,
    enc_norm_gain,
    mamba_in,
    mamba_bc,
    mamba_dt,
    dt_bias,
    decay_rate,
    skip_gain,
    gate_norm_gain,
    mamba_out,
    down_proj,
    attn_norm_gain,
    qkv_weight,
    out_weight,
    up_proj,
):
    axes = ("main", "sub")
    devices = lax.axis_size(axes)
    subs = lax.axis_size("sub")
    mains = lax.axis_size("main")
    main_id = lax.axis_index("main")
    rows, width = byte_states.shape
    heads = qkv_weight.shape[1]
    model = qkv_weight.shape[0]

    up_part = width // mains
    up_columns = lax.dynamic_slice_in_dim(up_proj, main_id * up_part, up_part, 1)
    out_up = dot(out_weight.reshape(heads * HD, model), up_columns).astype(BF)
    out_up, byte_states = lax.optimization_barrier((out_up, byte_states))
    out_up = jnp.concatenate(gather_sub(out_up, "sub"), 0)

    normed, x, bc, cum, late, chunk_states, decay, send = scan_states(
        byte_states,
        enc_norm_gain[None],
        mamba_in,
        mamba_bc,
        mamba_dt.T,
        dt_bias[None],
        decay_rate[None],
        devices,
    )
    send, out_up = lax.optimization_barrier((send, out_up))
    out_ups = gather_main(out_up, "main")
    parts = lax.all_to_all(send, axes, 0, 0, tiled=True)
    y, gate = scan_within(
        normed, mamba_in, x, bc, cum, late, skip_gain[None]
    )
    incoming = lax.all_to_all(state_prefix(parts), axes, 0, 0, tiled=True)
    incoming = incoming.reshape(HEAD_COUNT // 2, STATE, LANES)

    scaled_qkv = (attn_norm_gain[:, None] * qkv_weight.reshape(model, -1).astype(F32)).astype(BF)
    down_qkv = dot(down_proj, scaled_qkv).astype(BF)
    span_rank = jnp.cumsum(boundary_flags) - 1
    picked = jnp.where(boundary_flags == 1, span_rank, -1)
    encoded, span_rows = scan_finish(
        y,
        gate,
        bc,
        cum,
        incoming,
        chunk_states,
        decay,
        gate_norm_gain[None],
        mamba_out,
        byte_states,
        picked[None],
    )

    main_in = dot(span_rows, down_proj).astype(BF)
    wide = main_in.astype(F32)
    scale = lax.rsqrt(jnp.mean(wide * wide, -1, keepdims=True) + epsilon)
    sent_rows = (span_rows.astype(F32) * scale).astype(BF)
    sent_rows, *out_ups = lax.optimization_barrier((sent_rows, *out_ups))
    pieces = gather_sub(sent_rows, "sub")
    main_up = dot(main_in, up_proj)
    sub_index = sub_sources("sub")
    queries, kv = project_qkv(jnp.stack(sub_index).astype(jnp.int32), down_qkv, pieces, heads)
    slots = kv.shape[0]
    shards = [kv] + earlier_shards(kv, "main")
    sources = [main_id, main_id ^ 1]
    for k in range(2, mains, 2):
        sources += [main_id - k, (main_id ^ 1) - k]
    sources = [jnp.where(s < 0, mains, s) for s in sources]
    slot = jnp.arange(slots, dtype=jnp.int32)
    valid = slot[None] % CAP < jnp.repeat(
        span_counts.reshape(mains, subs), CAP, axis=1
    )
    bias = jnp.where(valid, 0.0, -1e30).astype(F32)
    index = jnp.stack([main_id] + sources).astype(jnp.int32)
    bias = jnp.take(bias, jnp.minimum(index[1:], mains - 1), axis=0)[:, None, :]
    heads_out = attention(index, queries, jnp.stack(shards), bias, heads)
    own_heads = lax.all_to_all(heads_out.reshape(subs, CAP, heads * HD), "sub", 0, 0)
    device_ids = jnp.arange(span_counts.shape[0], dtype=jnp.int32)
    device_id = main_id * subs + lax.axis_index("sub")
    own_count = jnp.sum(jnp.where(device_ids == device_id, span_counts, 0))
    span_up, edge_rows = project_up(
        jnp.stack(main_sources("main") + sub_index).astype(jnp.int32),
        main_up,
        own_heads,
        out_ups,
        own_count[None],
    )
    previous = lax.ppermute(edge_rows, axes, [(i, i + 1) for i in range(devices - 1)])[:2]
    table = jnp.concatenate([previous, span_up], 0)
    target = span_rank + 1
    spread = (target[:, None] == jnp.arange(CAP + 2)[None, :]).astype(BF)
    return (encoded.astype(F32) + dot(spread, table)).astype(BF)


def solution(mesh):
    return jax.shard_map(
        local,
        mesh=mesh,
        in_specs=(
            P(("main", "sub"), None),
            P(("main", "sub")),
            P(),
            P(),
            P(),
            P(),
            P(),
            P(),
            P(),
            P(),
            P(),
            P(),
            P(),
            P(),
            P(None, "sub", None),
            P("sub", None, None),
            P(),
        ),
        out_specs=P(("main", "sub"), None),
        check_vma=False,
    )
```

```python
import functools
import math

import jax
import jax.numpy as jnp
from jax import lax
from jax.experimental import pallas as pl
from jax.experimental.pallas import tpu as pltpu
from jax.sharding import PartitionSpec as P

INNER_WIDTH = 2048
HEAD_COUNT = 32
HEAD_WIDTH = 64
STATE = 128
HD = 128
CAP = 96
CHUNK = 128
LANES = 128
QUAD = 256
EXTRA = 16

epsilon = 1e-06
highest = lax.Precision.HIGHEST
LOG2E = math.log2(math.e)
BF = jnp.bfloat16
F32 = jnp.float32


def dot(a, b, **kw):
    return jnp.dot(a, b, preferred_element_type=F32, **kw)


def dot_t(a, b):
    return lax.dot_general(a, b, (((1,), (1,)), ((), ())), preferred_element_type=F32)


def silu(v):
    return v * jax.nn.sigmoid(v)


def params(**kw):
    return pltpu.CompilerParams(dimension_semantics=("arbitrary",), **kw)


def cost(us):
    return pl.CostEstimate(flops=int(us * 6e8), transcendentals=0, bytes_accessed=int(us * 3e6))


def whole(shape):
    rank = len(shape)
    return pl.BlockSpec(shape, lambda j: (0,) * rank)


def pair_lanes(columns, pair):
    rows = columns.shape[0]
    low = jnp.broadcast_to(columns[:, 2 * pair : 2 * pair + 1], (rows, LANES))
    high = jnp.broadcast_to(columns[:, 2 * pair + 1 : 2 * pair + 2], (rows, LANES))
    lane = lax.broadcasted_iota(jnp.int32, (rows, LANES), 1)
    return jnp.where(lane < HEAD_WIDTH, low, high)


def padded(row_ref):
    return jnp.concatenate([row_ref[...], jnp.zeros((1, LANES - HEAD_COUNT), F32)], 1)


def quad_columns(table, j):
    return pltpu.roll(table, (LANES - 4 * j) % LANES, 1)


def states_body(
    bytes_ref, gain_ref, wx_ref, wbc_ref, wdt_ref, bias_ref, rate_ref,
    normed_ref, x_ref, bc_ref, cum_ref, chunk_ref, late_ref, send_ref,
    bt_ref, weight_ref, total_ref,
):
    j = pl.program_id(0)
    rows = bytes_ref.shape[0]
    chunks = rows // CHUNK

    @pl.when(j == 0)
    def _():
        values = bytes_ref[...].astype(F32)
        scale = lax.rsqrt(jnp.mean(values * values, -1, keepdims=True) + epsilon)
        normed = (values * scale * gain_ref[...]).astype(BF)
        normed_ref[...] = normed
        bc = dot(normed, wbc_ref[...])
        bc_ref[...] = bc.astype(BF)
        spare = jnp.zeros((LANES - HEAD_COUNT, normed.shape[1]), BF)
        raw = dot_t(normed, jnp.concatenate([wdt_ref[...], spare], 0)) + padded(bias_ref)
        dt = jnp.maximum(raw, 0.0) + jnp.log1p(jnp.exp(-jnp.abs(raw)))
        step = dt * (-LOG2E * padded(rate_ref))
        row = lax.broadcasted_iota(jnp.int32, (CHUNK, CHUNK), 0)
        col = lax.broadcasted_iota(jnp.int32, (CHUNK, CHUNK), 1)
        lower = (row >= col).astype(F32)
        log_dt = jnp.log(dt) * LOG2E
        end = jnp.zeros((1, LANES), F32)
        lates = []
        for c in range(chunks):
            at = pl.ds(c * CHUNK, CHUNK)
            part = slice(c * CHUNK, (c + 1) * CHUNK)
            within = jnp.dot(lower, step[part], precision=highest, preferred_element_type=F32)
            cum = within + end
            cum_ref[at, :] = cum
            late = cum - log_dt[part]
            lates.append(late)
            turned = late.T
            for quad in range(HEAD_COUNT // 4):
                late_ref[quad, 0:4, at] = turned[4 * quad : 4 * quad + 4]
            end = cum[CHUNK - 1 :, :]
            chunk_ref[at, :] = jnp.exp2(end - late)
            bt_ref[:, at] = bc[part, :STATE].T.astype(BF)
        for c in range(chunks):
            weight_ref[pl.ds(c * CHUNK, CHUNK), :] = jnp.exp2(end - lates[c])
        total_ref[...] = jnp.broadcast_to(jnp.exp2(end), total_ref.shape)

    x = silu(dot(normed_ref[...], wx_ref[...]))
    x_ref[...] = x.astype(BF)
    weight = quad_columns(weight_ref[...], j)
    factor = quad_columns(total_ref[...], j)
    spread = jnp.concatenate([pair_lanes(weight, pair) for pair in range(2)], 1)
    state = dot(bt_ref[...], (x * spread).astype(BF))
    group = send_ref.shape[0] // 2
    piece = send_ref.shape[1] - EXTRA
    for pair in range(2):
        lanes = slice(pair * LANES, (pair + 1) * LANES)
        decay = pair_lanes(factor, pair)[:1]
        high = decay.astype(BF).astype(F32)
        row = lax.broadcasted_iota(jnp.int32, (EXTRA, LANES), 0)
        tail = jnp.where(row == 0, high, jnp.where(row == 1, decay - high, 0.0)).astype(BF)
        for d in range(group):
            part = slice(d * piece, (d + 1) * piece)
            send_ref[pair * group + d, :piece, :] = state[part, lanes].astype(BF)
            send_ref[pair * group + d, piece:, :] = tail


def scan_states(byte_states, gain, mamba_in, mamba_bc, mamba_dt, bias, rate, devices):
    rows, width = byte_states.shape
    steps = INNER_WIDTH // QUAD
    piece = INNER_WIDTH * STATE // (LANES * devices)
    return pl.pallas_call(
        states_body,
        grid=(steps,),
        in_specs=[
            whole((rows, width)),
            whole((1, width)),
            pl.BlockSpec((width, QUAD), lambda j: (0, j)),
            whole((width, 2 * STATE)),
            whole((HEAD_COUNT, width)),
            whole((1, HEAD_COUNT)),
            whole((1, HEAD_COUNT)),
        ],
        out_specs=[
            whole((rows, width)),
            pl.BlockSpec((rows, QUAD), lambda j: (0, j)),
            whole((rows, 2 * STATE)),
            whole((rows, LANES)),
            whole((rows, LANES)),
            whole((steps, 8, rows)),
            pl.BlockSpec((devices // steps, piece + EXTRA, LANES), lambda j: (j, 0, 0)),
        ],
        out_shape=[
            jax.ShapeDtypeStruct((rows, width), BF),
            jax.ShapeDtypeStruct((rows, INNER_WIDTH), BF),
            jax.ShapeDtypeStruct((rows, 2 * STATE), BF),
            jax.ShapeDtypeStruct((rows, LANES), F32),
            jax.ShapeDtypeStruct((rows, LANES), F32),
            jax.ShapeDtypeStruct((steps, 8, rows), F32),
            jax.ShapeDtypeStruct((devices, piece + EXTRA, LANES), BF),
        ],
        scratch_shapes=[
            pltpu.VMEM((STATE, rows), BF),
            pltpu.VMEM((rows, LANES), F32),
            pltpu.VMEM((8, LANES), F32),
        ],
        compiler_params=params(),
        cost_estimate=cost(9),
        name="scan_states",
    )(byte_states, gain, mamba_in, mamba_bc, mamba_dt, bias, rate)


def prefix_body(parts_ref, out_ref):
    devices, piece, _ = out_ref.shape
    state = jnp.zeros((piece, LANES), F32)
    for d in range(devices):
        out_ref[d] = state.astype(BF)
        tail = parts_ref[d, piece:, :].astype(F32)
        decay = tail[0:1] + tail[1:2]
        state = state * decay + parts_ref[d, :piece, :].astype(F32)


def state_prefix(parts):
    devices, rows, _ = parts.shape
    piece = rows - EXTRA
    return pl.pallas_call(
        prefix_body,
        grid=(1,),
        in_specs=[whole(parts.shape)],
        out_specs=whole((devices, piece, LANES)),
        out_shape=jax.ShapeDtypeStruct((devices, piece, LANES), BF),
        compiler_params=params(),
        cost_estimate=cost(2),
        name="state_prefix",
    )(parts)


def within_body(
    normed_ref, wg_ref, x_ref, bc_ref, cum_ref, chunk_ref, late_ref, skip_ref,
    yg_ref, grown_ref, contact_ref, bt_ref,
):
    j = pl.program_id(0)
    rows = normed_ref.shape[0]
    chunks = rows // CHUNK

    @pl.when(j == 0)
    def _():
        row = lax.broadcasted_iota(jnp.int32, (CHUNK, CHUNK), 0)
        col = lax.broadcasted_iota(jnp.int32, (CHUNK, CHUNK), 1)
        for c in range(chunks):
            at = pl.ds(c * CHUNK, CHUNK)
            contact = dot_t(bc_ref[at, STATE:], bc_ref[at, :STATE])
            contact_ref[c] = jnp.where(row >= col, contact, 0.0)
            bt_ref[c] = bc_ref[at, :STATE].astype(F32).T.astype(BF)

    gate = silu(dot(normed_ref[...], wg_ref[...]))
    cum = quad_columns(cum_ref[...], j)
    chunk = quad_columns(chunk_ref[...], j)
    skip = quad_columns(jnp.broadcast_to(padded(skip_ref), (8, LANES)), j)
    lane = lax.broadcasted_iota(jnp.int32, (CHUNK, LANES), 1)
    for pair in range(2):
        lanes = slice(pair * LANES, (pair + 1) * LANES)
        skips = pair_lanes(skip, pair)[:1]
        end = jnp.zeros((1, LANES), F32)
        state = None
        for c in range(chunks):
            at = pl.ds(c * CHUNK, CHUNK)
            part = slice(c * CHUNK, (c + 1) * CHUNK)
            weights = []
            for head in (2 * pair, 2 * pair + 1):
                gap = cum[part, head : head + 1] - late_ref[0, head : head + 1, at]
                weights.append((jnp.exp2(jnp.minimum(gap, 126.0)) * contact_ref[c]).astype(BF))
            packed = x_ref[at, lanes]
            zero = jnp.zeros_like(packed)
            stacked = jnp.concatenate(
                [jnp.where(lane < HEAD_WIDTH, packed, zero),
                 jnp.where(lane < HEAD_WIDTH, zero, packed)], 0
            )
            x = packed.astype(F32)
            y = dot(jnp.concatenate(weights, 1), stacked) + skips * x
            spread = pair_lanes(cum[part], pair)
            if c:
                y = y + dot(bc_ref[at, STATE:], state.astype(BF)) * jnp.exp2(spread - end)
            g = gate[part, lanes]
            yg_ref[at, lanes] = (y * g).astype(BF)
            grown_ref[at, lanes] = (jnp.exp2(spread) * g).astype(BF)
            if c + 1 < chunks:
                scaled = (x * pair_lanes(chunk[part], pair)).astype(BF)
                update = dot(bt_ref[c], scaled)
                last = spread[CHUNK - 1 :]
                state = update if c == 0 else state * jnp.exp2(last - end) + update
                end = last


def scan_within(normed, mamba_in, x, bc, cum, chunk, late, skip):
    rows, width = normed.shape
    chunks = rows // CHUNK
    steps = INNER_WIDTH // QUAD
    return pl.pallas_call(
        within_body,
        grid=(steps,),
        in_specs=[
            whole((rows, width)),
            pl.BlockSpec((width, QUAD), lambda j: (0, j + steps)),
            pl.BlockSpec((rows, QUAD), lambda j: (0, j)),
            whole((rows, 2 * STATE)),
            whole((rows, LANES)),
            whole((rows, LANES)),
            pl.BlockSpec((1, 8, rows), lambda j: (j, 0, 0)),
            whole((1, HEAD_COUNT)),
        ],
        out_specs=[pl.BlockSpec((rows, QUAD), lambda j: (0, j))] * 2,
        out_shape=[jax.ShapeDtypeStruct((rows, INNER_WIDTH), BF)] * 2,
        scratch_shapes=[
            pltpu.VMEM((chunks, CHUNK, CHUNK), F32),
            pltpu.VMEM((chunks, STATE, CHUNK), BF),
        ],
        compiler_params=params(),
        cost_estimate=cost(14),
        name="scan_within",
    )(normed, mamba_in, x, bc, cum, chunk, late, skip)


def finish_body(
    yg_ref, grown_ref, c_ref, incoming_ref, gain_ref, wo_ref, bytes_ref, rank_ref, down_ref,
    encoded_ref, main_ref, sent_ref, acc_ref, square_ref, weight_ref, sem,
):
    j = pl.program_id(0)
    rows = yg_ref.shape[0]

    @pl.when(j == 0)
    def _():
        pltpu.make_async_copy(down_ref, weight_ref, sem).start()
        square_ref[...] = jnp.zeros_like(square_ref)

    state = jnp.concatenate([incoming_ref[0], incoming_ref[1]], 1)
    carried = dot(c_ref[...], state)
    gated = yg_ref[...].astype(F32) + carried * grown_ref[...].astype(F32)
    square_ref[...] += gated[:, :LANES] * gated[:, :LANES] + gated[:, LANES:] * gated[:, LANES:]
    mixed = dot((gated * gain_ref[...]).astype(BF), wo_ref[...])

    @pl.when(j == 0)
    def _():
        acc_ref[...] = mixed

    @pl.when(j > 0)
    def _():
        acc_ref[...] += mixed

    @pl.when(j == pl.num_programs(0) - 1)
    def _():
        mean = jnp.sum(square_ref[...], -1, keepdims=True) * (1.0 / INNER_WIDTH)
        encoded = (bytes_ref[...].astype(F32) + acc_ref[...] * lax.rsqrt(mean + epsilon)).astype(BF)
        encoded_ref[...] = encoded
        slot = lax.broadcasted_iota(jnp.int32, (CAP, rows), 0)
        picker = jnp.where(rank_ref[...] == slot, 1.0, 0.0).astype(BF)
        spans = dot(picker, encoded)
        pltpu.make_async_copy(down_ref, weight_ref, sem).wait()
        main_in = dot(spans.astype(BF), weight_ref[...]).astype(BF)
        main_ref[...] = main_in
        wide = main_in.astype(F32)
        scale = lax.rsqrt(jnp.mean(wide * wide, -1, keepdims=True) + epsilon)
        sent_ref[...] = (spans * scale).astype(BF)


def scan_finish(yg, grown, bc, incoming, gain, mamba_out, byte_states, rank, down):
    rows, width = byte_states.shape
    steps = INNER_WIDTH // QUAD
    return pl.pallas_call(
        finish_body,
        grid=(steps,),
        in_specs=[
            pl.BlockSpec((rows, QUAD), lambda j: (0, j)),
            pl.BlockSpec((rows, QUAD), lambda j: (0, j)),
            pl.BlockSpec((rows, STATE), lambda j: (0, 1)),
            pl.BlockSpec((2, STATE, LANES), lambda j: (j, 0, 0)),
            pl.BlockSpec((1, QUAD), lambda j: (0, j)),
            pl.BlockSpec((QUAD, width), lambda j: (j, 0)),
            whole((rows, width)),
            whole((1, rows)),
            pl.BlockSpec(memory_space=pl.ANY),
        ],
        out_specs=[whole((rows, width)), whole((CAP, down.shape[1])), whole((CAP, width))],
        out_shape=[
            jax.ShapeDtypeStruct((rows, width), BF),
            jax.ShapeDtypeStruct((CAP, down.shape[1]), BF),
            jax.ShapeDtypeStruct((CAP, width), BF),
        ],
        scratch_shapes=[
            pltpu.VMEM((rows, width), F32),
            pltpu.VMEM((rows, LANES), F32),
            pltpu.VMEM(down.shape, BF),
            pltpu.SemaphoreType.DMA(()),
        ],
        compiler_params=params(),
        cost_estimate=cost(10),
        name="scan_finish",
    )(yg, grown, bc, incoming, gain, mamba_out, byte_states, rank, down)


def sub_grid(count):
    minor = 1
    while minor * minor * 4 <= count:
        minor *= 2
    return count // minor, minor


def sub_move(value, axis, dz, dx):
    count = lax.axis_size(axis)
    major, minor = sub_grid(count)
    route = []
    for i in range(count):
        z, x = divmod(i, minor)
        route.append((i, (z + dz) % major * minor + (x + dx) % minor))
    return lax.ppermute(value, axis, route)


def gather_columns(block, axis):
    major, _ = sub_grid(lax.axis_size(axis))
    return [block] + [sub_move(block, axis, dz, 0) for dz in range(1, major)]


def gather_rest(columns, axis):
    _, minor = sub_grid(lax.axis_size(axis))
    return columns + [sub_move(c, axis, 0, dx) for dx in range(1, minor) for c in columns]


def sub_sources(axis):
    count = lax.axis_size(axis)
    major, minor = sub_grid(count)
    me = lax.axis_index(axis)
    z, x = me // minor, me % minor
    return [(z - dz) % major * minor + (x - dx) % minor
            for dx in range(minor) for dz in range(major)]


def partner(value, axis):
    count = lax.axis_size(axis)
    return lax.ppermute(value, axis, [(i, i ^ 1) for i in range(count)])


def gather_main(block, axis):
    count = lax.axis_size(axis)
    near = [block] + [
        lax.ppermute(block, axis, [(i, (i + k) % count) for i in range(count)])
        for k in range(2, count, 2)
    ]
    near = jnp.stack(near)
    return near, partner(near, axis)


def main_sources(axis):
    count = lax.axis_size(axis)
    me = lax.axis_index(axis)
    return [(m - k) % count for m in (me, me ^ 1) for k in range(0, count, 2)]


def qkv_body(index_ref, *refs, first, heads):
    weight_ref, *pieces = refs[:-3]
    q_ref, kv_ref, rows_ref = refs[-3:]
    for p, piece in enumerate(pieces):
        rows_ref[index_ref[first + p]] = piece[...]
    count, cap, width = rows_ref.shape
    rows = rows_ref[...].reshape(count * cap, width)
    for h in range(heads):
        out = dot(rows, weight_ref[:, h * 3 * HD : (h + 1) * 3 * HD])
        q_ref[:, h * HD : (h + 1) * HD] = (out[:, :HD] * (HD**-0.5 * LOG2E)).astype(BF)
        kv_ref[:, h * 2 * HD : (h + 1) * 2 * HD] = out[:, HD:].astype(BF)


def vmem(count):
    return [pl.BlockSpec(memory_space=pltpu.VMEM)] * count


SCALARS = pl.BlockSpec(memory_space=pltpu.SMEM)


def project_qkv(index, first, weight, pieces):
    cap, width = pieces[0].shape
    slots = cap * len(pieces)
    heads = weight.shape[1] // (3 * HD)
    return pl.pallas_call(
        functools.partial(qkv_body, first=first, heads=heads),
        in_specs=[SCALARS] + vmem(1 + len(pieces)),
        out_specs=vmem(2),
        out_shape=[
            jax.ShapeDtypeStruct((slots, heads * HD), BF),
            jax.ShapeDtypeStruct((slots, heads * 2 * HD), BF),
        ],
        scratch_shapes=[pltpu.VMEM((len(pieces), cap, width), BF)],
        cost_estimate=cost(5),
        name="project_qkv",
    )(index, weight, *pieces)


def span_up_body(
    index_ref, edge_ref, main_up_ref, heads_ref, own_ref, other_ref, up_ref, edges_ref, columns_ref
):
    subs, cap, inner = heads_ref.shape
    half = own_ref.shape[0]
    mains = 2 * half
    flat = jnp.concatenate([heads_ref[index_ref[1 + mains + r]] for r in range(subs)], 1)
    for p in range(half):
        columns_ref[index_ref[1 + p]] = dot(flat, own_ref[p])
        columns_ref[index_ref[1 + half + p]] = dot(flat, other_ref[p])
    joined = jnp.concatenate([columns_ref[p] for p in range(mains)], 1)
    up = (main_up_ref[...] + joined).astype(BF)
    up_ref[...] = up
    slot = lax.broadcasted_iota(jnp.int32, (16, cap), 1)
    row = lax.broadcasted_iota(jnp.int32, (16, cap), 0)
    picker = jnp.where((slot == edge_ref[0] - 2 + row) & (row < 2), 1.0, 0.0).astype(BF)
    edges_ref[...] = dot(picker, up).astype(BF)


def project_up(index, main_up, heads, weights, own_count):
    cap, width = main_up.shape
    half, _, part = weights[0].shape
    return pl.pallas_call(
        span_up_body,
        in_specs=[SCALARS, SCALARS] + vmem(4),
        out_specs=vmem(2),
        out_shape=[
            jax.ShapeDtypeStruct((cap, width), BF),
            jax.ShapeDtypeStruct((16, width), BF),
        ],
        scratch_shapes=[pltpu.VMEM((2 * half, cap, part), F32)],
        cost_estimate=cost(5),
        name="project_up",
    )(index, own_count, main_up, heads, *weights)


BLOCK = 256


def scores_of(q, kv_ref, bias, head, span):
    return dot_t(q, kv_ref[:span, head * 2 * HD : head * 2 * HD + HD]) + bias[:, :span]


def mixed_of(numer, kv_ref, head, span):
    return dot(numer.astype(BF), kv_ref[:span, head * 2 * HD + HD : (head + 1) * 2 * HD])


def join(carry, q, kv_refs, biases, head):
    top, total, acc = carry
    slots = kv_refs[0].shape[0]
    scores = [scores_of(q, kv, bias, head, slots) for kv, bias in zip(kv_refs, biases)]
    new = top
    for s in scores:
        new = jnp.maximum(new, jnp.max(s, -1, keepdims=True))
    rescale = jnp.exp2(top - new)
    total, acc = total * rescale, acc * rescale
    for s, kv in zip(scores, kv_refs):
        numer = jnp.exp2(s - new)
        total = total + jnp.sum(numer, -1, keepdims=True)
        acc = acc + mixed_of(numer, kv, head, slots)
    return new, total, acc


def store(stats_ref, acc_ref, at, head, carry):
    top, total, acc = carry
    acc_ref[at, head * HD : (head + 1) * HD] = acc
    stats_ref[2 * head, at, :] = jnp.broadcast_to(top, acc.shape)
    stats_ref[2 * head + 1, at, :] = jnp.broadcast_to(total, acc.shape)


def near_body(index_ref, q_ref, kv_ref, other_ref, bias_ref, stats_ref, acc_ref):
    slots = q_ref.shape[0]
    heads = q_ref.shape[1] // HD
    mine = index_ref[0]

    def own(at, b, head):
        span = (b + 1) * BLOCK
        q = q_ref[at, head * HD : (head + 1) * HD]
        scores = scores_of(q, kv_ref, bias_ref[mine], head, span)
        row = lax.broadcasted_iota(jnp.int32, scores.shape, 0) + b * BLOCK
        col = lax.broadcasted_iota(jnp.int32, scores.shape, 1)
        scores = jnp.where(col <= row, scores, -2e30)
        top = jnp.max(scores, -1, keepdims=True)
        numer = jnp.exp2(scores - top)
        return top, jnp.sum(numer, -1, keepdims=True), mixed_of(numer, kv_ref, head, span)

    def run(paired):
        for b in range(slots // BLOCK):
            at = pl.ds(b * BLOCK, BLOCK)
            for head in range(heads):
                carry = own(at, b, head)
                if paired:
                    q = q_ref[at, head * HD : (head + 1) * HD]
                    carry = join(carry, q, [other_ref], [bias_ref[mine - 1]], head)
                store(stats_ref, acc_ref, at, head, carry)

    pl.when(mine % 2 == 1)(lambda: run(True))
    pl.when(mine % 2 == 0)(lambda: run(False))


def near_attention(index, q, kv, other, bias):
    slots, width = q.shape
    return pl.pallas_call(
        near_body,
        in_specs=[SCALARS] + vmem(4),
        out_specs=vmem(2),
        out_shape=[
            jax.ShapeDtypeStruct((2 * width // HD, slots, HD), F32),
            jax.ShapeDtypeStruct((slots, width), F32),
        ],
        cost_estimate=cost(9),
        name="near_attention",
    )(index, q, kv, other, bias)


def far_body(index_ref, q_ref, stats_in, acc_in, bias_ref, *refs):
    *pieces, out_ref, stats_ref, acc_ref = refs
    slots = q_ref.shape[0]
    heads = q_ref.shape[1] // HD
    mine = index_ref[0]
    steps = len(pieces) // 2

    def finish(at, head, carry):
        out_ref[at, head * HD : (head + 1) * HD] = (carry[2] / carry[1]).astype(BF)

    def each(refs, act):
        for b in range(slots // BLOCK):
            at = pl.ds(b * BLOCK, BLOCK)
            for head in range(heads):
                acc = refs[1][at, head * HD : (head + 1) * HD]
                act(at, head, (refs[0][2 * head, at, :1], refs[0][2 * head + 1, at, :1], acc))

    for k in range(steps):
        def act(at, head, carry, k=k):
            sources = (mine - 2 * (k + 1), mine + 1 - 2 * (mine % 2) - 2 * (k + 1))
            q = q_ref[at, head * HD : (head + 1) * HD]
            biases = [bias_ref[source] for source in sources]
            carry = join(carry, q, pieces[2 * k : 2 * k + 2], biases, head)
            last = mine < 2 * (k + 2)
            if k + 1 == steps:
                finish(at, head, carry)
            else:
                pl.when(last)(lambda: finish(at, head, carry))
                pl.when(jnp.logical_not(last))(lambda: store(stats_ref, acc_ref, at, head, carry))

        source_refs = (stats_in, acc_in) if k == 0 else (stats_ref, acc_ref)
        pl.when(mine >= 2 * (k + 1))(functools.partial(each, source_refs, act))

    pl.when(mine < 2)(functools.partial(each, (stats_in, acc_in), finish))


def far_attention(index, q, carry, bias, pieces):
    slots, width = q.shape
    return pl.pallas_call(
        far_body,
        in_specs=[SCALARS] + vmem(4 + len(pieces)),
        out_specs=vmem(1)[0],
        out_shape=jax.ShapeDtypeStruct((slots, width), BF),
        scratch_shapes=[pltpu.VMEM(carry[0].shape, F32), pltpu.VMEM((slots, width), F32)],
        cost_estimate=cost(9),
        name="far_attention",
    )(index, q, *carry, bias, *pieces)


def far_shards(kv, axis):
    count = lax.axis_size(axis)
    shifts = range(2, count, 2)
    return [lax.ppermute(kv, axis, [(i - k, i) for i in range(k, count)]) for k in shifts]


def local(
    byte_states,
    boundary_flags,
    span_counts,
    enc_norm_gain,
    mamba_in,
    mamba_bc,
    mamba_dt,
    dt_bias,
    decay_rate,
    skip_gain,
    gate_norm_gain,
    mamba_out,
    down_proj,
    attn_norm_gain,
    qkv_weight,
    out_weight,
    up_proj,
):
    axes = ("main", "sub")
    devices = lax.axis_size(axes)
    subs = lax.axis_size("sub")
    mains = lax.axis_size("main")
    main_id = lax.axis_index("main")
    rows, width = byte_states.shape
    heads = qkv_weight.shape[1]
    model = qkv_weight.shape[0]

    up_part = width // mains
    up_columns = lax.dynamic_slice_in_dim(up_proj, main_id * up_part, up_part, 1)
    out_up = dot(out_weight.reshape(heads * HD, model), up_columns).astype(BF)
    out_up, byte_states = lax.optimization_barrier((out_up, byte_states))
    out_up = gather_columns(out_up, "sub")

    normed, x, bc, cum, chunk, late, send = scan_states(
        byte_states,
        enc_norm_gain[None],
        mamba_in,
        mamba_bc,
        mamba_dt.T,
        dt_bias[None],
        decay_rate[None],
        devices,
    )
    send, flags, counts, *out_up = lax.optimization_barrier(
        (send, boundary_flags, span_counts, *out_up)
    )
    out_up = gather_rest([jnp.concatenate(out_up, 0)], "sub")
    parts = lax.all_to_all(send, axes, 0, 0, tiled=True)
    yg, grown = scan_within(normed, mamba_in, x, bc, cum, chunk, late, skip_gain[None])
    sub_index = sub_sources("sub")
    index = jnp.stack([main_id] + main_sources("main") + sub_index).astype(jnp.int32)
    slot = jnp.arange(subs * CAP, dtype=jnp.int32)
    valid = slot[None] % CAP < jnp.repeat(counts.reshape(mains, subs), CAP, axis=1)
    bias = jnp.where(valid, 0.0, -1e30).astype(F32)[:, None, :]
    span_rank = jnp.cumsum(flags) - 1
    picked = jnp.where(flags == 1, span_rank, -1)
    device_ids = jnp.arange(devices, dtype=jnp.int32)
    device_id = main_id * subs + lax.axis_index("sub")
    own_count = jnp.sum(jnp.where(device_ids == device_id, counts, 0))[None]
    parts, yg, grown, index, bias, picked, own_count, down, weight = lax.optimization_barrier(
        (parts, yg, grown, index, bias, picked, own_count, down_proj, qkv_weight)
    )
    incoming = lax.all_to_all(state_prefix(parts), axes, 0, 0, tiled=True)
    incoming = incoming.reshape(HEAD_COUNT // 2, STATE, LANES)
    scaled_down = (down.astype(F32) * attn_norm_gain[None]).astype(BF)
    down_qkv = dot(scaled_down, weight.reshape(model, -1)).astype(BF)
    incoming, down_qkv, *out_up = lax.optimization_barrier((incoming, down_qkv, *out_up))
    out_up = gather_main(jnp.concatenate(out_up, 0), "main")

    encoded, main_in, sent_rows = scan_finish(
        yg,
        grown,
        bc,
        incoming,
        gate_norm_gain[None],
        mamba_out,
        byte_states,
        picked[None],
        down_proj,
    )
    pieces = gather_rest(gather_columns(sent_rows, "sub"), "sub")
    main_up = dot(main_in, up_proj)
    queries, kv = project_qkv(index, 1 + mains, down_qkv, pieces)
    other = partner(kv, "main")
    far = far_shards(kv, "main")
    near = near_attention(index, queries, kv, other, bias)
    near, far = lax.optimization_barrier((near, far))
    far = [p for shard in far for p in (shard, partner(shard, "main"))]
    heads_out = far_attention(index, queries, near, bias, far)
    own_heads = lax.all_to_all(heads_out.reshape(subs, CAP, heads * HD), "sub", 0, 0)
    span_up, edge_rows = project_up(index, main_up, own_heads, out_up, own_count)
    previous = lax.ppermute(edge_rows, axes, [(i, i + 1) for i in range(devices - 1)])[:2]
    table = jnp.concatenate([previous, span_up], 0)
    target = span_rank + 1
    spread = (target[:, None] == jnp.arange(CAP + 2)[None, :]).astype(BF)
    return (encoded.astype(F32) + dot(spread, table)).astype(BF)


def solution(mesh):
    return jax.shard_map(
        local,
        mesh=mesh,
        in_specs=(
            P(("main", "sub"), None),
            P(("main", "sub")),
            P(),
            P(),
            P(),
            P(),
            P(),
            P(),
            P(),
            P(),
            P(),
            P(),
            P(),
            P(),
            P(None, "sub", None),
            P("sub", None, None),
            P(),
        ),
        out_specs=P(("main", "sub"), None),
        check_vma=False,
    )
```

```python
import functools
import math

import jax
import jax.numpy as jnp
from jax import lax
from jax.experimental import pallas as pl
from jax.experimental.pallas import tpu as pltpu
from jax.sharding import PartitionSpec as P


INNER_WIDTH = 2048
HEAD_COUNT = 32
HEAD_WIDTH = 64
STATE = 128
HD = 128
CAP = 96
CHUNK = 128
LANES = 128
QUAD = 256
STATE_STEP = 1024
FINISH_STEP = 1024
EXTRA = 16

epsilon = 1e-06
highest = lax.Precision.HIGHEST
LOG2E = math.log2(math.e)
BF = jnp.bfloat16
F32 = jnp.float32


def dot(a, b, **kw):
    return jnp.dot(a, b, preferred_element_type=F32, **kw)


def dot_t(a, b):
    return lax.dot_general(a, b, (((1,), (1,)), ((), ())), preferred_element_type=F32)


def silu(v):
    return v * jax.nn.sigmoid(v)


def params(**kw):
    return pltpu.CompilerParams(dimension_semantics=("arbitrary",), **kw)


def cost(us):
    return pl.CostEstimate(flops=int(us * 6e8), transcendentals=0, bytes_accessed=int(us * 3e6))


def whole(shape):
    rank = len(shape)
    return pl.BlockSpec(shape, lambda j: (0,) * rank)


def pair_lanes(columns, pair):
    rows = columns.shape[0]
    low = jnp.broadcast_to(columns[:, 2 * pair : 2 * pair + 1], (rows, LANES))
    high = jnp.broadcast_to(columns[:, 2 * pair + 1 : 2 * pair + 2], (rows, LANES))
    lane = lax.broadcasted_iota(jnp.int32, (rows, LANES), 1)
    return jnp.where(lane < HEAD_WIDTH, low, high)


def padded(row_ref):
    return jnp.concatenate([row_ref[...], jnp.zeros((1, LANES - HEAD_COUNT), F32)], 1)


def step_columns(table, j, width):
    return pltpu.roll(table, (LANES - width // HEAD_WIDTH * j) % LANES, 1)


def states_body(
    bytes_ref, gain_ref, wx_ref, wbc_ref, wdt_ref, bias_ref, rate_ref,
    normed_ref, x_ref, bc_ref, cum_ref, chunk_ref, late_ref, send_ref,
    bt_ref, weight_ref, total_ref,
):
    j = pl.program_id(0)
    rows = bytes_ref.shape[0]
    chunks = rows // CHUNK

    @pl.when(j == 0)
    def _():
        values = bytes_ref[...].astype(F32)
        scale = lax.rsqrt(jnp.mean(values * values, -1, keepdims=True) + epsilon)
        normed = (values * scale * gain_ref[...]).astype(BF)
        normed_ref[...] = normed
        bc = dot(normed, wbc_ref[...])
        bc_ref[...] = bc.astype(BF)
        spare = jnp.zeros((LANES - HEAD_COUNT, normed.shape[1]), BF)
        raw = dot_t(normed, jnp.concatenate([wdt_ref[...], spare], 0)) + padded(bias_ref)
        dt = jnp.maximum(raw, 0.0) + jnp.log1p(jnp.exp(-jnp.abs(raw)))
        step = dt * (-LOG2E * padded(rate_ref))
        row = lax.broadcasted_iota(jnp.int32, (CHUNK, CHUNK), 0)
        col = lax.broadcasted_iota(jnp.int32, (CHUNK, CHUNK), 1)
        lower = (row >= col).astype(F32)
        log_dt = jnp.log(dt) * LOG2E
        end = jnp.zeros((1, LANES), F32)
        lates = []
        for c in range(chunks):
            at = pl.ds(c * CHUNK, CHUNK)
            part = slice(c * CHUNK, (c + 1) * CHUNK)
            within = jnp.dot(lower, step[part], precision=highest, preferred_element_type=F32)
            cum = within + end
            cum_ref[at, :] = cum
            late = cum - log_dt[part]
            lates.append(late)
            turned = late.T
            for quad in range(HEAD_COUNT // 4):
                late_ref[quad, 0:4, at] = turned[4 * quad : 4 * quad + 4]
            end = cum[CHUNK - 1 :, :]
            chunk_ref[at, :] = jnp.exp2(end - late)
            bt_ref[:, at] = bc[part, :STATE].T.astype(BF)
        for c in range(chunks):
            weight_ref[pl.ds(c * CHUNK, CHUNK), :] = jnp.exp2(end - lates[c])
        total_ref[...] = jnp.broadcast_to(jnp.exp2(end), total_ref.shape)

    x = silu(dot(normed_ref[...], wx_ref[...]))
    x_ref[...] = x.astype(BF)
    weight = step_columns(weight_ref[...], j, STATE_STEP)
    factor = step_columns(total_ref[...], j, STATE_STEP)
    spread = jnp.concatenate([pair_lanes(weight, pair) for pair in range(STATE_STEP // LANES)], 1)
    state = dot(bt_ref[...], (x * spread).astype(BF))
    group = send_ref.shape[0] * LANES // STATE_STEP
    piece = send_ref.shape[1] - EXTRA
    for pair in range(STATE_STEP // LANES):
        lanes = slice(pair * LANES, (pair + 1) * LANES)
        decay = pair_lanes(factor, pair)[:1]
        high = decay.astype(BF).astype(F32)
        row = lax.broadcasted_iota(jnp.int32, (EXTRA, LANES), 0)
        tail = jnp.where(row == 0, high, jnp.where(row == 1, decay - high, 0.0)).astype(BF)
        for d in range(group):
            part = slice(d * piece, (d + 1) * piece)
            send_ref[pair * group + d, :piece, :] = state[part, lanes].astype(BF)
            send_ref[pair * group + d, piece:, :] = tail


def scan_states(byte_states, gain, mamba_in, mamba_bc, mamba_dt, bias, rate, devices):
    rows, width = byte_states.shape
    steps = INNER_WIDTH // STATE_STEP
    piece = INNER_WIDTH * STATE // (LANES * devices)
    return pl.pallas_call(
        states_body,
        grid=(steps,),
        in_specs=[
            whole((rows, width)),
            whole((1, width)),
            pl.BlockSpec((width, STATE_STEP), lambda j: (0, j)),
            whole((width, 2 * STATE)),
            whole((HEAD_COUNT, width)),
            whole((1, HEAD_COUNT)),
            whole((1, HEAD_COUNT)),
        ],
        out_specs=[
            whole((rows, width)),
            pl.BlockSpec((rows, STATE_STEP), lambda j: (0, j)),
            whole((rows, 2 * STATE)),
            whole((rows, LANES)),
            whole((rows, LANES)),
            whole((HEAD_COUNT // 4, 8, rows)),
            pl.BlockSpec((devices // steps, piece + EXTRA, LANES), lambda j: (j, 0, 0)),
        ],
        out_shape=[
            jax.ShapeDtypeStruct((rows, width), BF),
            jax.ShapeDtypeStruct((rows, INNER_WIDTH), BF),
            jax.ShapeDtypeStruct((rows, 2 * STATE), BF),
            jax.ShapeDtypeStruct((rows, LANES), F32),
            jax.ShapeDtypeStruct((rows, LANES), F32),
            jax.ShapeDtypeStruct((HEAD_COUNT // 4, 8, rows), F32),
            jax.ShapeDtypeStruct((devices, piece + EXTRA, LANES), BF),
        ],
        scratch_shapes=[
            pltpu.VMEM((STATE, rows), BF),
            pltpu.VMEM((rows, LANES), F32),
            pltpu.VMEM((8, LANES), F32),
        ],
        compiler_params=params(),
        cost_estimate=cost(9),
        name="scan_states",
    )(byte_states, gain, mamba_in, mamba_bc, mamba_dt, bias, rate)


def prefix_body(parts_ref, out_ref):
    devices, piece, _ = out_ref.shape
    state = jnp.zeros((piece, LANES), F32)
    for d in range(devices):
        out_ref[d] = state.astype(BF)
        tail = parts_ref[d, piece:, :].astype(F32)
        decay = tail[0:1] + tail[1:2]
        state = state * decay + parts_ref[d, :piece, :].astype(F32)


def state_prefix(parts):
    devices, rows, _ = parts.shape
    piece = rows - EXTRA
    return pl.pallas_call(
        prefix_body,
        grid=(1,),
        in_specs=[whole(parts.shape)],
        out_specs=whole((devices, piece, LANES)),
        out_shape=jax.ShapeDtypeStruct((devices, piece, LANES), BF),
        compiler_params=params(),
        cost_estimate=cost(2),
        name="state_prefix",
    )(parts)


def within_body(
    normed_ref, wg_ref, x_ref, bc_ref, cum_ref, chunk_ref, late_ref, skip_ref,
    yg_ref, grown_ref, contact_ref, bt_ref,
):
    j = pl.program_id(0)
    rows = normed_ref.shape[0]
    chunks = rows // CHUNK

    @pl.when(j == 0)
    def _():
        row = lax.broadcasted_iota(jnp.int32, (CHUNK, CHUNK), 0)
        col = lax.broadcasted_iota(jnp.int32, (CHUNK, CHUNK), 1)
        for c in range(chunks):
            at = pl.ds(c * CHUNK, CHUNK)
            contact = dot_t(bc_ref[at, STATE:], bc_ref[at, :STATE])
            contact_ref[c] = jnp.where(row >= col, contact, 0.0)
            bt_ref[c] = bc_ref[at, :STATE].astype(F32).T.astype(BF)

    gate = silu(dot(normed_ref[...], wg_ref[...]))
    cum = step_columns(cum_ref[...], j, QUAD)
    chunk = step_columns(chunk_ref[...], j, QUAD)
    skip = step_columns(jnp.broadcast_to(padded(skip_ref), (8, LANES)), j, QUAD)
    lane = lax.broadcasted_iota(jnp.int32, (CHUNK, LANES), 1)
    for pair in range(2):
        lanes = slice(pair * LANES, (pair + 1) * LANES)
        skips = pair_lanes(skip, pair)[:1]
        end = jnp.zeros((1, LANES), F32)
        state = None
        for c in range(chunks):
            at = pl.ds(c * CHUNK, CHUNK)
            part = slice(c * CHUNK, (c + 1) * CHUNK)
            weights = []
            for head in (2 * pair, 2 * pair + 1):
                gap = cum[part, head : head + 1] - late_ref[0, head : head + 1, at]
                weights.append((jnp.exp2(jnp.minimum(gap, 126.0)) * contact_ref[c]).astype(BF))
            packed = x_ref[at, lanes]
            zero = jnp.zeros_like(packed)
            stacked = jnp.concatenate(
                [jnp.where(lane < HEAD_WIDTH, packed, zero),
                 jnp.where(lane < HEAD_WIDTH, zero, packed)], 0
            )
            x = packed.astype(F32)
            y = dot(jnp.concatenate(weights, 1), stacked) + skips * x
            spread = pair_lanes(cum[part], pair)
            if c:
                y = y + dot(bc_ref[at, STATE:], state.astype(BF)) * jnp.exp2(spread - end)
            g = gate[part, lanes]
            yg_ref[at, lanes] = (y * g).astype(BF)
            grown_ref[at, lanes] = (jnp.exp2(spread) * g).astype(BF)
            if c + 1 < chunks:
                scaled = (x * pair_lanes(chunk[part], pair)).astype(BF)
                update = dot(bt_ref[c], scaled)
                last = spread[CHUNK - 1 :]
                state = update if c == 0 else state * jnp.exp2(last - end) + update
                end = last


def scan_within(normed, mamba_in, x, bc, cum, chunk, late, skip):
    rows, width = normed.shape
    chunks = rows // CHUNK
    steps = INNER_WIDTH // QUAD
    return pl.pallas_call(
        within_body,
        grid=(steps,),
        in_specs=[
            whole((rows, width)),
            pl.BlockSpec((width, QUAD), lambda j: (0, j + steps)),
            pl.BlockSpec((rows, QUAD), lambda j: (0, j)),
            whole((rows, 2 * STATE)),
            whole((rows, LANES)),
            whole((rows, LANES)),
            pl.BlockSpec((1, 8, rows), lambda j: (j, 0, 0)),
            whole((1, HEAD_COUNT)),
        ],
        out_specs=[pl.BlockSpec((rows, QUAD), lambda j: (0, j))] * 2,
        out_shape=[jax.ShapeDtypeStruct((rows, INNER_WIDTH), BF)] * 2,
        scratch_shapes=[
            pltpu.VMEM((chunks, CHUNK, CHUNK), F32),
            pltpu.VMEM((chunks, STATE, CHUNK), BF),
        ],
        compiler_params=params(),
        cost_estimate=cost(14),
        name="scan_within",
    )(normed, mamba_in, x, bc, cum, chunk, late, skip)


def finish_body(
    yg_ref, grown_ref, c_ref, incoming_ref, gain_ref, wo_ref, bytes_ref, rank_ref, down_ref,
    encoded_ref, main_ref, sent_ref, acc_ref, square_ref, weight_ref, sem,
):
    j = pl.program_id(0)
    rows = yg_ref.shape[0]

    @pl.when(j == 0)
    def _():
        pltpu.make_async_copy(down_ref, weight_ref, sem).start()
        square_ref[...] = jnp.zeros_like(square_ref)

    state = jnp.concatenate([incoming_ref[p] for p in range(incoming_ref.shape[0])], 1)
    carried = dot(c_ref[...], state)
    gated = yg_ref[...].astype(F32) + carried * grown_ref[...].astype(F32)
    parts = [gated[:, p : p + LANES] for p in range(0, FINISH_STEP, LANES)]
    square_ref[...] += sum(part * part for part in parts)
    mixed = dot((gated * gain_ref[...]).astype(BF), wo_ref[...])

    @pl.when(j == 0)
    def _():
        acc_ref[...] = mixed

    @pl.when(j > 0)
    def _():
        acc_ref[...] += mixed

    @pl.when(j == pl.num_programs(0) - 1)
    def _():
        mean = jnp.sum(square_ref[...], -1, keepdims=True) * (1.0 / INNER_WIDTH)
        encoded = (bytes_ref[...].astype(F32) + acc_ref[...] * lax.rsqrt(mean + epsilon)).astype(BF)
        encoded_ref[...] = encoded
        slot = lax.broadcasted_iota(jnp.int32, (CAP, rows), 0)
        picker = jnp.where(rank_ref[...] == slot, 1.0, 0.0).astype(BF)
        spans = dot(picker, encoded)
        pltpu.make_async_copy(down_ref, weight_ref, sem).wait()
        main_in = dot(spans.astype(BF), weight_ref[...]).astype(BF)
        main_ref[...] = main_in
        wide = main_in.astype(F32)
        scale = lax.rsqrt(jnp.mean(wide * wide, -1, keepdims=True) + epsilon)
        sent_ref[...] = (spans * scale).astype(BF)


def scan_finish(yg, grown, bc, incoming, gain, mamba_out, byte_states, rank, down):
    rows, width = byte_states.shape
    steps = INNER_WIDTH // FINISH_STEP
    return pl.pallas_call(
        finish_body,
        grid=(steps,),
        in_specs=[
            pl.BlockSpec((rows, FINISH_STEP), lambda j: (0, j)),
            pl.BlockSpec((rows, FINISH_STEP), lambda j: (0, j)),
            pl.BlockSpec((rows, STATE), lambda j: (0, 1)),
            pl.BlockSpec((FINISH_STEP // LANES, STATE, LANES), lambda j: (j, 0, 0)),
            pl.BlockSpec((1, FINISH_STEP), lambda j: (0, j)),
            pl.BlockSpec((FINISH_STEP, width), lambda j: (j, 0)),
            whole((rows, width)),
            whole((1, rows)),
            pl.BlockSpec(memory_space=pl.ANY),
        ],
        out_specs=[whole((rows, width)), whole((CAP, down.shape[1])), whole((CAP, width))],
        out_shape=[
            jax.ShapeDtypeStruct((rows, width), BF),
            jax.ShapeDtypeStruct((CAP, down.shape[1]), BF),
            jax.ShapeDtypeStruct((CAP, width), BF),
        ],
        scratch_shapes=[
            pltpu.VMEM((rows, width), F32),
            pltpu.VMEM((rows, LANES), F32),
            pltpu.VMEM(down.shape, BF),
            pltpu.SemaphoreType.DMA(()),
        ],
        compiler_params=params(),
        cost_estimate=cost(10),
        name="scan_finish",
    )(yg, grown, bc, incoming, gain, mamba_out, byte_states, rank, down)


def sub_grid(count):
    minor = 1
    while minor * minor * 4 <= count:
        minor *= 2
    return count // minor, minor


def sub_move(value, axis, dz, dx):
    count = lax.axis_size(axis)
    major, minor = sub_grid(count)
    route = []
    for i in range(count):
        z, x = divmod(i, minor)
        route.append((i, (z + dz) % major * minor + (x + dx) % minor))
    return lax.ppermute(value, axis, route)


def gather_columns(block, axis):
    major, _ = sub_grid(lax.axis_size(axis))
    return [block] + [sub_move(block, axis, dz, 0) for dz in range(1, major)]


def gather_rest(columns, axis):
    _, minor = sub_grid(lax.axis_size(axis))
    return columns + [sub_move(c, axis, 0, dx) for dx in range(1, minor) for c in columns]


def sub_sources(axis):
    count = lax.axis_size(axis)
    major, minor = sub_grid(count)
    me = lax.axis_index(axis)
    z, x = me // minor, me % minor
    return [(z - dz) % major * minor + (x - dx) % minor
            for dx in range(minor) for dz in range(major)]


def partner(value, axis):
    count = lax.axis_size(axis)
    return lax.ppermute(value, axis, [(i, i ^ 1) for i in range(count)])


def gather_main(block, axis):
    count = lax.axis_size(axis)
    near = [block] + [
        lax.ppermute(block, axis, [(i, (i + k) % count) for i in range(count)])
        for k in range(2, count, 2)
    ]
    near = jnp.stack(near)
    return near, partner(near, axis)


def main_sources(axis):
    count = lax.axis_size(axis)
    me = lax.axis_index(axis)
    return [(m - k) % count for m in (me, me ^ 1) for k in range(0, count, 2)]


def qkv_body(weight_ref, *refs):
    *pieces, q_ref, kv_ref = refs
    rows = jnp.concatenate([piece[...] for piece in pieces], 0)
    for h in range(weight_ref.shape[1] // (3 * HD)):
        out = dot(rows, weight_ref[:, h * 3 * HD : (h + 1) * 3 * HD])
        q_ref[:, h * HD : (h + 1) * HD] = (out[:, :HD] * (HD**-0.5 * LOG2E)).astype(BF)
        kv_ref[:, h * 2 * HD : (h + 1) * 2 * HD] = out[:, HD:].astype(BF)


def vmem(count):
    return [pl.BlockSpec(memory_space=pltpu.VMEM)] * count


SCALARS = pl.BlockSpec(memory_space=pltpu.SMEM)


def project_qkv(weight, pieces):
    slots = pieces[0].shape[0] * len(pieces)
    heads = weight.shape[1] // (3 * HD)
    return pl.pallas_call(
        qkv_body,
        in_specs=vmem(1 + len(pieces)),
        out_specs=vmem(2),
        out_shape=[
            jax.ShapeDtypeStruct((slots, heads * HD), BF),
            jax.ShapeDtypeStruct((slots, heads * 2 * HD), BF),
        ],
        cost_estimate=cost(4),
        name="project_qkv",
    )(weight, *pieces)


def place(out_ref, index_ref, parts):
    first = index_ref.shape[0] - out_ref.shape[0] // CAP
    for part in parts:
        for p in range(part.shape[0] // CAP):
            at = pl.multiple_of(index_ref[first] * CAP, 32)
            out_ref[pl.ds(at, CAP), :] = part[p * CAP : (p + 1) * CAP, :]
            first += 1


def span_up_body(
    index_ref, edge_ref, main_up_ref, heads_ref, own_ref, other_ref, up_ref, edges_ref, columns_ref
):
    subs, cap, _ = heads_ref.shape
    half = own_ref.shape[0]
    mains = 2 * half
    flat = jnp.concatenate([heads_ref[index_ref[1 + mains + r]] for r in range(subs)], 1)
    for p in range(half):
        columns_ref[index_ref[1 + p]] = dot(flat, own_ref[p])
        columns_ref[index_ref[1 + half + p]] = dot(flat, other_ref[p])
    joined = jnp.concatenate([columns_ref[p] for p in range(mains)], 1)
    up = (main_up_ref[...] + joined).astype(BF)
    up_ref[...] = up
    slot = lax.broadcasted_iota(jnp.int32, (16, cap), 1)
    row = lax.broadcasted_iota(jnp.int32, (16, cap), 0)
    picker = jnp.where((slot == edge_ref[0] - 2 + row) & (row < 2), 1.0, 0.0).astype(BF)
    edges_ref[...] = dot(picker, up).astype(BF)


def project_up(index, main_up, heads, weights, own_count):
    cap, width = main_up.shape
    half, _, part = weights[0].shape
    return pl.pallas_call(
        span_up_body,
        in_specs=[SCALARS, SCALARS] + vmem(4),
        out_specs=vmem(2),
        out_shape=[
            jax.ShapeDtypeStruct((cap, width), BF),
            jax.ShapeDtypeStruct((16, width), BF),
        ],
        scratch_shapes=[pltpu.VMEM((2 * half, cap, part), F32)],
        cost_estimate=cost(5),
        name="project_up",
    )(index, own_count, main_up, heads, *weights)


BLOCK = 256


def scores_of(q, kv_ref, bias, head, span):
    return dot_t(q, kv_ref[:span, head * 2 * HD : head * 2 * HD + HD]) + bias[:, :span]


def mixed_of(numer, kv_ref, head, span):
    return dot(numer.astype(BF), kv_ref[:span, head * 2 * HD + HD : (head + 1) * 2 * HD])


def join(carry, q, kv_refs, biases, head):
    top, total, acc = carry
    slots = kv_refs[0].shape[0]
    scores = [scores_of(q, kv, bias, head, slots) for kv, bias in zip(kv_refs, biases)]
    new = top
    for s in scores:
        new = jnp.maximum(new, jnp.max(s, -1, keepdims=True))
    rescale = jnp.exp2(top - new)
    total, acc = total * rescale, acc * rescale
    for s, kv in zip(scores, kv_refs):
        numer = jnp.exp2(s - new)
        total = total + jnp.sum(numer, -1, keepdims=True)
        acc = acc + mixed_of(numer, kv, head, slots)
    return new, total, acc


def store(stats_ref, acc_ref, at, head, carry):
    top, total, acc = carry
    acc_ref[at, head * HD : (head + 1) * HD] = acc
    stats_ref[2 * head, at, :] = jnp.broadcast_to(top, acc.shape)
    stats_ref[2 * head + 1, at, :] = jnp.broadcast_to(total, acc.shape)


def near_body(index_ref, bias_ref, *refs):
    *parts, q_ref, stats_ref, acc_ref, kv_ref, other_ref = refs
    count = len(parts) // 3
    place(q_ref, index_ref, parts[:count])
    place(kv_ref, index_ref, parts[count : 2 * count])
    pl.when(index_ref[0] % 2 == 1)(lambda: place(other_ref, index_ref, parts[2 * count :]))
    slots = q_ref.shape[0]
    heads = q_ref.shape[1] // HD
    mine = index_ref[0]

    def own(at, b, head):
        span = (b + 1) * BLOCK
        q = q_ref[at, head * HD : (head + 1) * HD]
        scores = scores_of(q, kv_ref, bias_ref[mine], head, span)
        row = lax.broadcasted_iota(jnp.int32, scores.shape, 0) + b * BLOCK
        col = lax.broadcasted_iota(jnp.int32, scores.shape, 1)
        scores = jnp.where(col <= row, scores, -2e30)
        top = jnp.max(scores, -1, keepdims=True)
        numer = jnp.exp2(scores - top)
        return top, jnp.sum(numer, -1, keepdims=True), mixed_of(numer, kv_ref, head, span)

    def run(paired):
        for b in range(slots // BLOCK):
            at = pl.ds(b * BLOCK, BLOCK)
            for head in range(heads):
                carry = own(at, b, head)
                if paired:
                    q = q_ref[at, head * HD : (head + 1) * HD]
                    carry = join(carry, q, [other_ref], [bias_ref[mine - 1]], head)
                store(stats_ref, acc_ref, at, head, carry)

    pl.when(mine % 2 == 1)(lambda: run(True))
    pl.when(mine % 2 == 0)(lambda: run(False))


def near_attention(index, bias, queries, keys, others):
    slots = bias.shape[2]
    width = queries[0].shape[1]
    parts = [*queries, *keys, *others]
    return pl.pallas_call(
        near_body,
        in_specs=[SCALARS] + vmem(1 + len(parts)),
        out_specs=vmem(3),
        out_shape=[
            jax.ShapeDtypeStruct((slots, width), BF),
            jax.ShapeDtypeStruct((2 * width // HD, slots, HD), F32),
            jax.ShapeDtypeStruct((slots, width), F32),
        ],
        scratch_shapes=[pltpu.VMEM((slots, 2 * width), BF)] * 2,
        cost_estimate=cost(9),
        name="near_attention",
    )(index, bias, *parts)


def far_body(index_ref, q_ref, stats_in, acc_in, bias_ref, *refs, shards):
    parts, (out_ref, stats_ref, acc_ref, *pieces) = refs[: -3 - shards], refs[-3 - shards :]
    slots = q_ref.shape[0]
    heads = q_ref.shape[1] // HD
    mine = index_ref[0]
    steps = shards // 2
    count = len(parts) // shards

    @pl.when(mine >= 2)
    def _():
        for p, piece in enumerate(pieces):
            place(piece, index_ref, parts[p * count : (p + 1) * count])

    def finish(at, head, carry):
        out_ref[at, head * HD : (head + 1) * HD] = (carry[2] / carry[1]).astype(BF)

    def each(refs, act):
        for b in range(slots // BLOCK):
            at = pl.ds(b * BLOCK, BLOCK)
            for head in range(heads):
                acc = refs[1][at, head * HD : (head + 1) * HD]
                act(at, head, (refs[0][2 * head, at, :1], refs[0][2 * head + 1, at, :1], acc))

    for k in range(steps):
        def act(at, head, carry, k=k):
            sources = (mine - 2 * (k + 1), mine + 1 - 2 * (mine % 2) - 2 * (k + 1))
            q = q_ref[at, head * HD : (head + 1) * HD]
            biases = [bias_ref[source] for source in sources]
            carry = join(carry, q, pieces[2 * k : 2 * k + 2], biases, head)
            last = mine < 2 * (k + 2)
            if k + 1 == steps:
                finish(at, head, carry)
            else:
                pl.when(last)(lambda: finish(at, head, carry))
                pl.when(jnp.logical_not(last))(lambda: store(stats_ref, acc_ref, at, head, carry))

        source_refs = (stats_in, acc_in) if k == 0 else (stats_ref, acc_ref)
        pl.when(mine >= 2 * (k + 1))(functools.partial(each, source_refs, act))

    pl.when(mine < 2)(functools.partial(each, (stats_in, acc_in), finish))


def far_attention(index, q, stats, acc, bias, shards):
    slots, width = q.shape
    parts = [part for shard in shards for part in shard]
    return pl.pallas_call(
        functools.partial(far_body, shards=len(shards)),
        in_specs=[SCALARS] + vmem(4 + len(parts)),
        out_specs=vmem(1)[0],
        out_shape=jax.ShapeDtypeStruct((slots, width), BF),
        scratch_shapes=[pltpu.VMEM(stats.shape, F32), pltpu.VMEM((slots, width), F32)]
        + [pltpu.VMEM((slots, 2 * width), BF)] * len(shards),
        cost_estimate=cost(9),
        name="far_attention",
    )(index, q, stats, acc, bias, *parts)


def far_shards(kv, axis):
    count = lax.axis_size(axis)
    shifts = range(2, count, 2)
    return [lax.ppermute(kv, axis, [(i - k, i) for i in range(k, count)]) for k in shifts]


def local(
    byte_states,
    boundary_flags,
    span_counts,
    enc_norm_gain,
    mamba_in,
    mamba_bc,
    mamba_dt,
    dt_bias,
    decay_rate,
    skip_gain,
    gate_norm_gain,
    mamba_out,
    down_proj,
    attn_norm_gain,
    qkv_weight,
    out_weight,
    up_proj,
):
    axes = ("main", "sub")
    devices = lax.axis_size(axes)
    subs = lax.axis_size("sub")
    mains = lax.axis_size("main")
    main_id = lax.axis_index("main")
    _, width = byte_states.shape
    heads = qkv_weight.shape[1]
    model = qkv_weight.shape[0]

    up_part = width // mains
    up_columns = lax.dynamic_slice_in_dim(up_proj, main_id * up_part, up_part, 1)
    out_up = dot(out_weight.reshape(heads * HD, model), up_columns).astype(BF)
    out_up, byte_states = lax.optimization_barrier((out_up, byte_states))
    out_up = gather_columns(out_up, "sub")

    normed, x, bc, cum, chunk, late, send = scan_states(
        byte_states,
        enc_norm_gain[None],
        mamba_in,
        mamba_bc,
        mamba_dt.T,
        dt_bias[None],
        decay_rate[None],
        devices,
    )
    send, flags, counts, *out_up = lax.optimization_barrier(
        (send, boundary_flags, span_counts, *out_up)
    )
    out_up = gather_rest([jnp.concatenate(out_up, 0)], "sub")
    parts = lax.all_to_all(send, axes, 0, 0, tiled=True)
    yg, grown = scan_within(normed, mamba_in, x, bc, cum, chunk, late, skip_gain[None])
    sub_index = sub_sources("sub")
    index = jnp.stack([main_id] + main_sources("main") + sub_index).astype(jnp.int32)
    slot = jnp.arange(subs * CAP, dtype=jnp.int32)
    valid = slot[None] % CAP < jnp.repeat(counts.reshape(mains, subs), CAP, axis=1)
    bias = jnp.where(valid, 0.0, -1e30).astype(F32)[:, None, :]
    span_rank = jnp.cumsum(flags) - 1
    picked = jnp.where(flags == 1, span_rank, -1)
    device_ids = jnp.arange(devices, dtype=jnp.int32)
    device_id = main_id * subs + lax.axis_index("sub")
    own_count = jnp.sum(jnp.where(device_ids == device_id, counts, 0))[None]
    parts, yg, grown, index, bias, picked, own_count, down, weight, *out_up = (
        lax.optimization_barrier(
            (parts, yg, grown, index, bias, picked, own_count, down_proj, qkv_weight, *out_up)
        )
    )
    out_up = gather_main(jnp.concatenate(out_up, 0), "main")
    incoming = lax.all_to_all(state_prefix(parts), axes, 0, 0, tiled=True)
    incoming = incoming.reshape(HEAD_COUNT // 2, STATE, LANES)
    scaled_down = (down.astype(F32) * attn_norm_gain[None]).astype(BF)
    down_qkv = dot(scaled_down, weight.reshape(model, -1)).astype(BF)
    incoming, down_qkv = lax.optimization_barrier((incoming, down_qkv))

    encoded, main_in, sent_rows = scan_finish(
        yg,
        grown,
        bc,
        incoming,
        gate_norm_gain[None],
        mamba_out,
        byte_states,
        picked[None],
        down_proj,
    )
    columns = gather_columns(sent_rows, "sub")
    pieces = gather_rest(columns, "sub")
    main_up = dot(main_in, up_proj)
    groups = [pieces[: len(columns)], pieces[len(columns) :]]
    projected = []
    for group in groups:
        projected.append(project_qkv(down_qkv, group))
    keys = [kv for _, kv in projected]
    others = [partner(kv, "main") for kv in keys]
    far = []
    for kv in keys:
        far.append(far_shards(kv, "main"))
    q, stats, acc = near_attention(index, bias, [q for q, _ in projected], keys, others)
    stats, far = lax.optimization_barrier((stats, far))
    shards = []
    for k in range(mains // 2 - 1):
        direct = [group[k] for group in far]
        shards += [direct, [partner(part, "main") for part in direct]]
    heads_out = far_attention(index, q, stats, acc, bias, shards)
    own_heads = lax.all_to_all(heads_out.reshape(subs, CAP, heads * HD), "sub", 0, 0)
    span_up, edge_rows = project_up(index, main_up, own_heads, out_up, own_count)
    previous = lax.ppermute(edge_rows, axes, [(i, i + 1) for i in range(devices - 1)])[:2]
    table = jnp.concatenate([previous, span_up], 0)
    target = span_rank + 1
    spread = (target[:, None] == jnp.arange(CAP + 2)[None, :]).astype(BF)
    return (encoded.astype(F32) + dot(spread, table)).astype(BF)


def solution(mesh):
    return jax.shard_map(
        local,
        mesh=mesh,
        in_specs=(
            P(("main", "sub"), None),
            P(("main", "sub")),
            P(),
            P(),
            P(),
            P(),
            P(),
            P(),
            P(),
            P(),
            P(),
            P(),
            P(),
            P(),
            P(None, "sub", None),
            P("sub", None, None),
            P(),
        ),
        out_specs=P(("main", "sub"), None),
        check_vma=False,
    )
```

```python
import functools
import math

import jax
import jax.numpy as jnp
from jax import lax
from jax.experimental import pallas as pl
from jax.experimental.pallas import tpu as pltpu
from jax.sharding import PartitionSpec as P


INNER_WIDTH = 2048
HEAD_COUNT = 32
HEAD_WIDTH = 64
STATE = 128
HD = 128
CAP = 96
CHUNK = 128
LANES = 128
WITHIN_STEP = 512
STATE_STEP = 1024
FINISH_STEP = 1024
EXTRA = 16

epsilon = 1e-06
highest = lax.Precision.HIGHEST
LOG2E = math.log2(math.e)
BF = jnp.bfloat16
F32 = jnp.float32


def dot(a, b, **kw):
    return jnp.dot(a, b, preferred_element_type=F32, **kw)


def dot_t(a, b):
    return lax.dot_general(a, b, (((1,), (1,)), ((), ())), preferred_element_type=F32)


def silu(v):
    return v * jax.nn.sigmoid(v)


def params(**kw):
    return pltpu.CompilerParams(dimension_semantics=("arbitrary",), **kw)


def cost(us):
    return pl.CostEstimate(flops=int(us * 6e8), transcendentals=0, bytes_accessed=int(us * 3e6))


def whole(shape):
    rank = len(shape)
    return pl.BlockSpec(shape, lambda j: (0,) * rank)


def pair_lanes(columns, pair):
    rows = columns.shape[0]
    low = jnp.broadcast_to(columns[:, 2 * pair : 2 * pair + 1], (rows, LANES))
    high = jnp.broadcast_to(columns[:, 2 * pair + 1 : 2 * pair + 2], (rows, LANES))
    lane = lax.broadcasted_iota(jnp.int32, (rows, LANES), 1)
    return jnp.where(lane < HEAD_WIDTH, low, high)


def padded(row_ref):
    return jnp.concatenate([row_ref[...], jnp.zeros((1, LANES - HEAD_COUNT), F32)], 1)


def step_columns(table, j, width):
    return pltpu.roll(table, (LANES - width // HEAD_WIDTH * j) % LANES, 1)


def states_body(
    bytes_ref, gain_ref, wx_ref, wbc_ref, wdt_ref, bias_ref, rate_ref,
    normed_ref, x_ref, bc_ref, cum_ref, chunk_ref, late_ref, send_ref,
    bt_ref, weight_ref, total_ref,
):
    j = pl.program_id(0)
    rows = bytes_ref.shape[0]
    chunks = rows // CHUNK

    @pl.when(j == 0)
    def _():
        values = bytes_ref[...].astype(F32)
        scale = lax.rsqrt(jnp.mean(values * values, -1, keepdims=True) + epsilon)
        normed = (values * scale * gain_ref[...]).astype(BF)
        normed_ref[...] = normed
        bc = dot(normed, wbc_ref[...])
        bc_ref[...] = bc.astype(BF)
        spare = jnp.zeros((LANES - HEAD_COUNT, normed.shape[1]), BF)
        raw = dot_t(normed, jnp.concatenate([wdt_ref[...], spare], 0)) + padded(bias_ref)
        dt = jnp.maximum(raw, 0.0) + jnp.log1p(jnp.exp(-jnp.abs(raw)))
        step = dt * (-LOG2E * padded(rate_ref))
        row = lax.broadcasted_iota(jnp.int32, (CHUNK, CHUNK), 0)
        col = lax.broadcasted_iota(jnp.int32, (CHUNK, CHUNK), 1)
        lower = (row >= col).astype(F32)
        log_dt = jnp.log(dt) * LOG2E
        end = jnp.zeros((1, LANES), F32)
        lates = []
        for c in range(chunks):
            at = pl.ds(c * CHUNK, CHUNK)
            part = slice(c * CHUNK, (c + 1) * CHUNK)
            within = jnp.dot(lower, step[part], precision=highest, preferred_element_type=F32)
            cum = within + end
            cum_ref[at, :] = cum
            late = cum - log_dt[part]
            lates.append(late)
            turned = late.T
            for quad in range(HEAD_COUNT // 4):
                late_ref[quad, 0:4, at] = turned[4 * quad : 4 * quad + 4]
            end = cum[CHUNK - 1 :, :]
            chunk_ref[at, :] = jnp.exp2(end - late)
            bt_ref[:, at] = bc[part, :STATE].T.astype(BF)
        for c in range(chunks):
            weight_ref[pl.ds(c * CHUNK, CHUNK), :] = jnp.exp2(end - lates[c])
        total_ref[...] = jnp.broadcast_to(jnp.exp2(end), total_ref.shape)

    x = silu(dot(normed_ref[...], wx_ref[...]))
    x_ref[...] = x.astype(BF)
    weight = step_columns(weight_ref[...], j, STATE_STEP)
    factor = step_columns(total_ref[...], j, STATE_STEP)
    spread = jnp.concatenate([pair_lanes(weight, pair) for pair in range(STATE_STEP // LANES)], 1)
    state = dot(bt_ref[...], (x * spread).astype(BF))
    group = send_ref.shape[0] * LANES // STATE_STEP
    piece = send_ref.shape[1] - EXTRA
    for pair in range(STATE_STEP // LANES):
        lanes = slice(pair * LANES, (pair + 1) * LANES)
        decay = pair_lanes(factor, pair)[:1]
        high = decay.astype(BF).astype(F32)
        row = lax.broadcasted_iota(jnp.int32, (EXTRA, LANES), 0)
        tail = jnp.where(row == 0, high, jnp.where(row == 1, decay - high, 0.0)).astype(BF)
        for d in range(group):
            part = slice(d * piece, (d + 1) * piece)
            send_ref[pair * group + d, :piece, :] = state[part, lanes].astype(BF)
            send_ref[pair * group + d, piece:, :] = tail


def scan_states(byte_states, gain, mamba_in, mamba_bc, mamba_dt, bias, rate, devices):
    rows, width = byte_states.shape
    steps = INNER_WIDTH // STATE_STEP
    piece = INNER_WIDTH * STATE // (LANES * devices)
    return pl.pallas_call(
        states_body,
        grid=(steps,),
        in_specs=[
            whole((rows, width)),
            whole((1, width)),
            pl.BlockSpec((width, STATE_STEP), lambda j: (0, j)),
            whole((width, 2 * STATE)),
            whole((HEAD_COUNT, width)),
            whole((1, HEAD_COUNT)),
            whole((1, HEAD_COUNT)),
        ],
        out_specs=[
            whole((rows, width)),
            pl.BlockSpec((rows, STATE_STEP), lambda j: (0, j)),
            whole((rows, 2 * STATE)),
            whole((rows, LANES)),
            whole((rows, LANES)),
            whole((HEAD_COUNT // 4, 8, rows)),
            pl.BlockSpec((devices // steps, piece + EXTRA, LANES), lambda j: (j, 0, 0)),
        ],
        out_shape=[
            jax.ShapeDtypeStruct((rows, width), BF),
            jax.ShapeDtypeStruct((rows, INNER_WIDTH), BF),
            jax.ShapeDtypeStruct((rows, 2 * STATE), BF),
            jax.ShapeDtypeStruct((rows, LANES), F32),
            jax.ShapeDtypeStruct((rows, LANES), F32),
            jax.ShapeDtypeStruct((HEAD_COUNT // 4, 8, rows), F32),
            jax.ShapeDtypeStruct((devices, piece + EXTRA, LANES), BF),
        ],
        scratch_shapes=[
            pltpu.VMEM((STATE, rows), BF),
            pltpu.VMEM((rows, LANES), F32),
            pltpu.VMEM((8, LANES), F32),
        ],
        compiler_params=params(),
        cost_estimate=cost(9),
        name="scan_states",
    )(byte_states, gain, mamba_in, mamba_bc, mamba_dt, bias, rate)


def prefix_body(parts_ref, out_ref):
    devices, piece, _ = out_ref.shape
    state = jnp.zeros((piece, LANES), F32)
    for d in range(devices):
        out_ref[d] = state.astype(BF)
        tail = parts_ref[d, piece:, :].astype(F32)
        decay = tail[0:1] + tail[1:2]
        state = state * decay + parts_ref[d, :piece, :].astype(F32)


def state_prefix(parts):
    devices, rows, _ = parts.shape
    piece = rows - EXTRA
    return pl.pallas_call(
        prefix_body,
        grid=(1,),
        in_specs=[whole(parts.shape)],
        out_specs=whole((devices, piece, LANES)),
        out_shape=jax.ShapeDtypeStruct((devices, piece, LANES), BF),
        compiler_params=params(),
        cost_estimate=cost(2),
        name="state_prefix",
    )(parts)


def within_body(
    normed_ref, wg_ref, x_ref, bc_ref, cum_ref, chunk_ref, late_ref, skip_ref,
    yg_ref, grown_ref, contact_ref, bt_ref,
):
    j = pl.program_id(0)
    rows = normed_ref.shape[0]
    chunks = rows // CHUNK

    @pl.when(j == 0)
    def _():
        row = lax.broadcasted_iota(jnp.int32, (CHUNK, CHUNK), 0)
        col = lax.broadcasted_iota(jnp.int32, (CHUNK, CHUNK), 1)
        for c in range(chunks):
            at = pl.ds(c * CHUNK, CHUNK)
            contact = dot_t(bc_ref[at, STATE:], bc_ref[at, :STATE])
            contact_ref[c] = jnp.where(row >= col, contact, 0.0)
            bt_ref[c] = bc_ref[at, :STATE].astype(F32).T.astype(BF)

    gate = silu(dot(normed_ref[...], wg_ref[...]))
    cum = step_columns(cum_ref[...], j, WITHIN_STEP)
    chunk = step_columns(chunk_ref[...], j, WITHIN_STEP)
    skip = step_columns(jnp.broadcast_to(padded(skip_ref), (8, LANES)), j, WITHIN_STEP)
    lane = lax.broadcasted_iota(jnp.int32, (CHUNK, LANES), 1)
    for pair in range(WITHIN_STEP // LANES):
        lanes = slice(pair * LANES, (pair + 1) * LANES)
        skips = pair_lanes(skip, pair)[:1]
        end = jnp.zeros((1, LANES), F32)
        state = None
        for c in range(chunks):
            at = pl.ds(c * CHUNK, CHUNK)
            part = slice(c * CHUNK, (c + 1) * CHUNK)
            weights = []
            for head in (2 * pair, 2 * pair + 1):
                gap = cum[part, head : head + 1] - late_ref[head // 4, head % 4 : head % 4 + 1, at]
                weights.append((jnp.exp2(jnp.minimum(gap, 126.0)) * contact_ref[c]).astype(BF))
            packed = x_ref[at, lanes]
            zero = jnp.zeros_like(packed)
            stacked = jnp.concatenate(
                [jnp.where(lane < HEAD_WIDTH, packed, zero),
                 jnp.where(lane < HEAD_WIDTH, zero, packed)], 0
            )
            x = packed.astype(F32)
            y = dot(jnp.concatenate(weights, 1), stacked) + skips * x
            spread = pair_lanes(cum[part], pair)
            if c:
                y = y + dot(bc_ref[at, STATE:], state.astype(BF)) * jnp.exp2(spread - end)
            g = gate[part, lanes]
            yg_ref[at, lanes] = (y * g).astype(BF)
            grown_ref[at, lanes] = (jnp.exp2(spread) * g).astype(BF)
            if c + 1 < chunks:
                scaled = (x * pair_lanes(chunk[part], pair)).astype(BF)
                update = dot(bt_ref[c], scaled)
                last = spread[CHUNK - 1 :]
                state = update if c == 0 else state * jnp.exp2(last - end) + update
                end = last


def scan_within(normed, mamba_in, x, bc, cum, chunk, late, skip):
    rows, width = normed.shape
    chunks = rows // CHUNK
    steps = INNER_WIDTH // WITHIN_STEP
    return pl.pallas_call(
        within_body,
        grid=(steps,),
        in_specs=[
            whole((rows, width)),
            pl.BlockSpec((width, WITHIN_STEP), lambda j: (0, j + steps)),
            pl.BlockSpec((rows, WITHIN_STEP), lambda j: (0, j)),
            whole((rows, 2 * STATE)),
            whole((rows, LANES)),
            whole((rows, LANES)),
            pl.BlockSpec((WITHIN_STEP // 256, 8, rows), lambda j: (j, 0, 0)),
            whole((1, HEAD_COUNT)),
        ],
        out_specs=[pl.BlockSpec((rows, WITHIN_STEP), lambda j: (0, j))] * 2,
        out_shape=[jax.ShapeDtypeStruct((rows, INNER_WIDTH), BF)] * 2,
        scratch_shapes=[
            pltpu.VMEM((chunks, CHUNK, CHUNK), F32),
            pltpu.VMEM((chunks, STATE, CHUNK), BF),
        ],
        compiler_params=params(),
        cost_estimate=cost(14),
        name="scan_within",
    )(normed, mamba_in, x, bc, cum, chunk, late, skip)


def finish_body(
    yg_ref, grown_ref, c_ref, incoming_ref, gain_ref, wo_ref, bytes_ref, rank_ref, down_ref,
    encoded_ref, main_ref, sent_ref, acc_ref, square_ref, weight_ref, sem,
):
    j = pl.program_id(0)
    rows = yg_ref.shape[0]

    @pl.when(j == 0)
    def _():
        pltpu.make_async_copy(down_ref, weight_ref, sem).start()
        square_ref[...] = jnp.zeros_like(square_ref)

    state = jnp.concatenate([incoming_ref[p] for p in range(incoming_ref.shape[0])], 1)
    carried = dot(c_ref[...], state)
    gated = yg_ref[...].astype(F32) + carried * grown_ref[...].astype(F32)
    parts = [gated[:, p : p + LANES] for p in range(0, FINISH_STEP, LANES)]
    square_ref[...] += sum(part * part for part in parts)
    mixed = dot((gated * gain_ref[...]).astype(BF), wo_ref[...])

    @pl.when(j == 0)
    def _():
        acc_ref[...] = mixed

    @pl.when(j > 0)
    def _():
        acc_ref[...] += mixed

    @pl.when(j == pl.num_programs(0) - 1)
    def _():
        mean = jnp.sum(square_ref[...], -1, keepdims=True) * (1.0 / INNER_WIDTH)
        encoded = (bytes_ref[...].astype(F32) + acc_ref[...] * lax.rsqrt(mean + epsilon)).astype(BF)
        encoded_ref[...] = encoded
        slot = lax.broadcasted_iota(jnp.int32, (CAP, rows), 0)
        picker = jnp.where(rank_ref[...] == slot, 1.0, 0.0).astype(BF)
        spans = dot(picker, encoded)
        pltpu.make_async_copy(down_ref, weight_ref, sem).wait()
        main_in = dot(spans.astype(BF), weight_ref[...]).astype(BF)
        main_ref[...] = main_in
        wide = main_in.astype(F32)
        scale = lax.rsqrt(jnp.mean(wide * wide, -1, keepdims=True) + epsilon)
        sent_ref[...] = (spans * scale).astype(BF)


def scan_finish(yg, grown, bc, incoming, gain, mamba_out, byte_states, rank, down):
    rows, width = byte_states.shape
    steps = INNER_WIDTH // FINISH_STEP
    return pl.pallas_call(
        finish_body,
        grid=(steps,),
        in_specs=[
            pl.BlockSpec((rows, FINISH_STEP), lambda j: (0, j)),
            pl.BlockSpec((rows, FINISH_STEP), lambda j: (0, j)),
            pl.BlockSpec((rows, STATE), lambda j: (0, 1)),
            pl.BlockSpec((FINISH_STEP // LANES, STATE, LANES), lambda j: (j, 0, 0)),
            pl.BlockSpec((1, FINISH_STEP), lambda j: (0, j)),
            pl.BlockSpec((FINISH_STEP, width), lambda j: (j, 0)),
            whole((rows, width)),
            whole((1, rows)),
            pl.BlockSpec(memory_space=pl.ANY),
        ],
        out_specs=[whole((rows, width)), whole((CAP, down.shape[1])), whole((CAP, width))],
        out_shape=[
            jax.ShapeDtypeStruct((rows, width), BF),
            jax.ShapeDtypeStruct((CAP, down.shape[1]), BF),
            jax.ShapeDtypeStruct((CAP, width), BF),
        ],
        scratch_shapes=[
            pltpu.VMEM((rows, width), F32),
            pltpu.VMEM((rows, LANES), F32),
            pltpu.VMEM(down.shape, BF),
            pltpu.SemaphoreType.DMA(()),
        ],
        compiler_params=params(),
        cost_estimate=cost(10),
        name="scan_finish",
    )(yg, grown, bc, incoming, gain, mamba_out, byte_states, rank, down)


def sub_grid(count):
    minor = 1
    while minor * minor * 4 <= count:
        minor *= 2
    return count // minor, minor


def sub_move(value, axis, dz, dx):
    count = lax.axis_size(axis)
    major, minor = sub_grid(count)
    route = []
    for i in range(count):
        z, x = divmod(i, minor)
        route.append((i, (z + dz) % major * minor + (x + dx) % minor))
    return lax.ppermute(value, axis, route)


def places(major):
    return [0, 1, major - 1] + list(range(2, major - 1))


def gather_columns(block, axis):
    major, _ = sub_grid(lax.axis_size(axis))
    return [block] + [sub_move(block, axis, dz, 0) for dz in places(major)[1:]]


def forward(value, axis):
    _, minor = sub_grid(lax.axis_size(axis))
    return [sub_move(value, axis, 0, dx) for dx in range(1, minor)]


def gather_rest(columns, axis):
    moved = [forward(c, axis) for c in columns]
    return columns + [piece for dx in zip(*moved) for piece in dx]


def sub_sources(axis):
    count = lax.axis_size(axis)
    major, minor = sub_grid(count)
    me = lax.axis_index(axis)
    z, x = me // minor, me % minor
    return [(z - dz) % major * minor + (x - dx) % minor
            for dx in range(minor) for dz in places(major)]


def partner(value, axis):
    count = lax.axis_size(axis)
    return lax.ppermute(value, axis, [(i, i ^ 1) for i in range(count)])


def gather_main(block, axis):
    count = lax.axis_size(axis)
    near = [block] + [
        lax.ppermute(block, axis, [(i, (i + k) % count) for i in range(count)])
        for k in range(2, count, 2)
    ]
    return near + [partner(part, axis) for part in near]


def main_sources(axis):
    count = lax.axis_size(axis)
    me = lax.axis_index(axis)
    return [(m - k) % count for m in (me, me ^ 1) for k in range(0, count, 2)]


def qkv_body(weight_ref, *refs):
    *pieces, q_ref, kv_ref = refs
    rows = jnp.concatenate([piece[...] for piece in pieces], 0)
    for h in range(weight_ref.shape[1] // (3 * HD)):
        out = dot(rows, weight_ref[:, h * 3 * HD : (h + 1) * 3 * HD])
        q_ref[:, h * HD : (h + 1) * HD] = (out[:, :HD] * (HD**-0.5 * LOG2E)).astype(BF)
        kv_ref[:, h * 2 * HD : (h + 1) * 2 * HD] = out[:, HD:].astype(BF)


def vmem(count):
    return [pl.BlockSpec(memory_space=pltpu.VMEM)] * count


SCALARS = pl.BlockSpec(memory_space=pltpu.SMEM)


def project_qkv(weight, pieces):
    slots = pieces[0].shape[0] * len(pieces)
    heads = weight.shape[1] // (3 * HD)
    return pl.pallas_call(
        qkv_body,
        in_specs=vmem(1 + len(pieces)),
        out_specs=vmem(2),
        out_shape=[
            jax.ShapeDtypeStruct((slots, heads * HD), BF),
            jax.ShapeDtypeStruct((slots, heads * 2 * HD), BF),
        ],
        cost_estimate=cost(4),
        name="project_qkv",
    )(weight, *pieces)


def place(out_ref, index_ref, parts):
    first = index_ref.shape[0] - out_ref.shape[0] // CAP
    for part in parts:
        for p in range(part.shape[0] // CAP):
            at = pl.multiple_of(index_ref[first] * CAP, 32)
            out_ref[pl.ds(at, CAP), :] = part[p * CAP : (p + 1) * CAP, :]
            first += 1


def span_up_body(index_ref, edge_ref, main_up_ref, heads_ref, *refs):
    *weights, up_ref, edges_ref, columns_ref = refs
    subs, cap, _ = heads_ref.shape
    mains = columns_ref.shape[0]
    depth = weights[0].shape[0]
    flat = jnp.concatenate([heads_ref[index_ref[1 + mains + r]] for r in range(subs)], 1)
    for p in range(mains):
        part = 0.0
        for g, weight in enumerate(weights[p::mains]):
            part = part + dot(flat[:, g * depth : (g + 1) * depth], weight[...])
        columns_ref[index_ref[1 + p]] = part
    joined = jnp.concatenate([columns_ref[p] for p in range(mains)], 1)
    up = (main_up_ref[...] + joined).astype(BF)
    up_ref[...] = up
    slot = lax.broadcasted_iota(jnp.int32, (16, cap), 1)
    row = lax.broadcasted_iota(jnp.int32, (16, cap), 0)
    picker = jnp.where((slot == edge_ref[0] - 2 + row) & (row < 2), 1.0, 0.0).astype(BF)
    edges_ref[...] = dot(picker, up).astype(BF)


def project_up(index, main_up, heads, groups, own_count):
    cap, width = main_up.shape
    part = groups[0][0].shape[1]
    weights = [weight for group in groups for weight in group]
    return pl.pallas_call(
        span_up_body,
        in_specs=[SCALARS, SCALARS] + vmem(2 + len(weights)),
        out_specs=vmem(2),
        out_shape=[
            jax.ShapeDtypeStruct((cap, width), BF),
            jax.ShapeDtypeStruct((16, width), BF),
        ],
        scratch_shapes=[pltpu.VMEM((len(groups[0]), cap, part), F32)],
        cost_estimate=cost(5),
        name="project_up",
    )(index, own_count, main_up, heads, *weights)


BLOCK = 384


def scores_of(q, kv_ref, bias, head, span):
    return dot_t(q, kv_ref[:span, head * 2 * HD : head * 2 * HD + HD]) + bias[:, :span]


def mixed_of(numer, kv_ref, head, span):
    return dot(numer.astype(BF), kv_ref[:span, head * 2 * HD + HD : (head + 1) * 2 * HD])


def join(carry, q, kv_refs, biases, head):
    top, total, acc = carry
    slots = kv_refs[0].shape[0]
    scores = [scores_of(q, kv, bias, head, slots) for kv, bias in zip(kv_refs, biases)]
    new = top
    for s in scores:
        new = jnp.maximum(new, jnp.max(s, -1, keepdims=True))
    rescale = jnp.exp2(top - new)
    total, acc = total * rescale, acc * rescale
    for s, kv in zip(scores, kv_refs):
        numer = jnp.exp2(s - new)
        total = total + jnp.sum(numer, -1, keepdims=True)
        acc = acc + mixed_of(numer, kv, head, slots)
    return new, total, acc


def store(stats_ref, acc_ref, at, head, carry):
    top, total, acc = carry
    acc_ref[at, head * HD : (head + 1) * HD] = acc
    stats_ref[2 * head, at, :] = jnp.broadcast_to(top, acc.shape)
    stats_ref[2 * head + 1, at, :] = jnp.broadcast_to(total, acc.shape)


def near_body(index_ref, bias_ref, *refs):
    *parts, q_ref, stats_ref, acc_ref, kv_ref, other_ref = refs
    count = len(parts) // 3
    place(q_ref, index_ref, parts[:count])
    place(kv_ref, index_ref, parts[count : 2 * count])
    pl.when(index_ref[0] % 2 == 1)(lambda: place(other_ref, index_ref, parts[2 * count :]))
    slots = q_ref.shape[0]
    heads = q_ref.shape[1] // HD
    mine = index_ref[0]

    def own(at, b, head):
        span = (b + 1) * BLOCK
        q = q_ref[at, head * HD : (head + 1) * HD]
        scores = scores_of(q, kv_ref, bias_ref[mine], head, span)
        row = lax.broadcasted_iota(jnp.int32, scores.shape, 0) + b * BLOCK
        col = lax.broadcasted_iota(jnp.int32, scores.shape, 1)
        scores = jnp.where(col <= row, scores, -2e30)
        top = jnp.max(scores, -1, keepdims=True)
        numer = jnp.exp2(scores - top)
        return top, jnp.sum(numer, -1, keepdims=True), mixed_of(numer, kv_ref, head, span)

    def run(paired):
        for b in range(slots // BLOCK):
            at = pl.ds(b * BLOCK, BLOCK)
            for head in range(heads):
                carry = own(at, b, head)
                if paired:
                    q = q_ref[at, head * HD : (head + 1) * HD]
                    carry = join(carry, q, [other_ref], [bias_ref[mine - 1]], head)
                store(stats_ref, acc_ref, at, head, carry)

    pl.when(mine % 2 == 1)(lambda: run(True))
    pl.when(mine % 2 == 0)(lambda: run(False))


def near_attention(index, bias, queries, keys, others):
    slots = bias.shape[2]
    width = queries[0].shape[1]
    parts = [*queries, *keys, *others]
    return pl.pallas_call(
        near_body,
        in_specs=[SCALARS] + vmem(1 + len(parts)),
        out_specs=vmem(3),
        out_shape=[
            jax.ShapeDtypeStruct((slots, width), BF),
            jax.ShapeDtypeStruct((2 * width // HD, slots, HD), F32),
            jax.ShapeDtypeStruct((slots, width), F32),
        ],
        scratch_shapes=[pltpu.VMEM((slots, 2 * width), BF)] * 2,
        cost_estimate=cost(9),
        name="near_attention",
    )(index, bias, *parts)


def far_body(index_ref, q_ref, stats_in, acc_in, bias_ref, *refs, shards):
    parts, (out_ref, stats_ref, acc_ref, *pieces) = refs[: -3 - shards], refs[-3 - shards :]
    slots = q_ref.shape[0]
    heads = q_ref.shape[1] // HD
    mine = index_ref[0]
    steps = shards // 2
    count = len(parts) // shards

    @pl.when(mine >= 2)
    def _():
        for p, piece in enumerate(pieces):
            place(piece, index_ref, parts[p * count : (p + 1) * count])

    def finish(at, head, carry):
        out_ref[at, head * HD : (head + 1) * HD] = (carry[2] / carry[1]).astype(BF)

    def each(refs, act):
        for b in range(slots // BLOCK):
            at = pl.ds(b * BLOCK, BLOCK)
            for head in range(heads):
                acc = refs[1][at, head * HD : (head + 1) * HD]
                act(at, head, (refs[0][2 * head, at, :1], refs[0][2 * head + 1, at, :1], acc))

    for k in range(steps):
        def act(at, head, carry, k=k):
            sources = (mine - 2 * (k + 1), mine + 1 - 2 * (mine % 2) - 2 * (k + 1))
            q = q_ref[at, head * HD : (head + 1) * HD]
            biases = [bias_ref[source] for source in sources]
            carry = join(carry, q, pieces[2 * k : 2 * k + 2], biases, head)
            last = mine < 2 * (k + 2)
            if k + 1 == steps:
                finish(at, head, carry)
            else:
                pl.when(last)(lambda: finish(at, head, carry))
                pl.when(jnp.logical_not(last))(lambda: store(stats_ref, acc_ref, at, head, carry))

        source_refs = (stats_in, acc_in) if k == 0 else (stats_ref, acc_ref)
        pl.when(mine >= 2 * (k + 1))(functools.partial(each, source_refs, act))

    pl.when(mine < 2)(functools.partial(each, (stats_in, acc_in), finish))


def far_attention(index, q, stats, acc, bias, shards):
    slots, width = q.shape
    parts = [part for shard in shards for part in shard]
    return pl.pallas_call(
        functools.partial(far_body, shards=len(shards)),
        in_specs=[SCALARS] + vmem(4 + len(parts)),
        out_specs=vmem(1)[0],
        out_shape=jax.ShapeDtypeStruct((slots, width), BF),
        scratch_shapes=[pltpu.VMEM(stats.shape, F32), pltpu.VMEM((slots, width), F32)]
        + [pltpu.VMEM((slots, 2 * width), BF)] * len(shards),
        cost_estimate=cost(9),
        name="far_attention",
    )(index, q, stats, acc, bias, *parts)


def far_shards(kv, axis):
    count = lax.axis_size(axis)
    shifts = range(2, count, 2)
    return [lax.ppermute(kv, axis, [(i - k, i) for i in range(k, count)]) for k in shifts]


def local(
    byte_states,
    boundary_flags,
    span_counts,
    enc_norm_gain,
    mamba_in,
    mamba_bc,
    mamba_dt,
    dt_bias,
    decay_rate,
    skip_gain,
    gate_norm_gain,
    mamba_out,
    down_proj,
    attn_norm_gain,
    qkv_weight,
    out_weight,
    up_proj,
):
    axes = ("main", "sub")
    devices = lax.axis_size(axes)
    subs = lax.axis_size("sub")
    mains = lax.axis_size("main")
    main_id = lax.axis_index("main")
    _, width = byte_states.shape
    heads = qkv_weight.shape[1]
    model = qkv_weight.shape[0]

    normed, x, bc, cum, chunk, late, send = scan_states(
        byte_states,
        enc_norm_gain[None],
        mamba_in,
        mamba_bc,
        mamba_dt.T,
        dt_bias[None],
        decay_rate[None],
        devices,
    )
    send, weight, up, out, main_id = lax.optimization_barrier(
        (send, qkv_weight, up_proj, out_weight, main_id)
    )
    parts = lax.all_to_all(send, axes, 0, 0, tiled=True)
    weight = weight.reshape(model, -1)
    up_part = width // mains
    up_columns = lax.dynamic_slice_in_dim(up, main_id * up_part, up_part, 1)
    out_up = dot(out.reshape(heads * HD, model), up_columns).astype(BF)
    yg, grown = scan_within(normed, mamba_in, x, bc, cum, chunk, late, skip_gain[None])
    parts, yg, grown, down, weight, flags, out_up = lax.optimization_barrier(
        (parts, yg, grown, down_proj, weight, boundary_flags, out_up)
    )
    incoming = lax.all_to_all(state_prefix(parts), axes, 0, 0, tiled=True)
    incoming = incoming.reshape(HEAD_COUNT // 2, STATE, LANES)
    scaled_down = (down.astype(F32) * attn_norm_gain[None]).astype(BF)
    down_qkv = dot(scaled_down, weight).astype(BF)
    span_rank = jnp.cumsum(flags) - 1
    picked = jnp.where(flags == 1, span_rank, -1)
    incoming, down_qkv, picked, out_up = lax.optimization_barrier(
        (incoming, down_qkv, picked, out_up)
    )
    out_up = gather_columns(out_up, "sub")

    encoded, main_in, sent_rows = scan_finish(
        yg,
        grown,
        bc,
        incoming,
        gate_norm_gain[None],
        mamba_out,
        byte_states,
        picked[None],
        down_proj,
    )
    sent_rows, counts, main_id, *out_up = lax.optimization_barrier(
        (sent_rows, span_counts, main_id, *out_up)
    )
    out_up = jnp.concatenate(out_up, 0)
    out_ups = [gather_main(out_up, "main")]
    columns = gather_columns(sent_rows, "sub")
    sub_index = sub_sources("sub")
    index = jnp.stack([main_id] + main_sources("main") + sub_index).astype(jnp.int32)
    slot = jnp.arange(subs * CAP, dtype=jnp.int32)
    valid = slot[None] % CAP < jnp.repeat(counts.reshape(mains, subs), CAP, axis=1)
    bias = jnp.where(valid, 0.0, -1e30).astype(F32)[:, None, :]
    device_ids = jnp.arange(devices, dtype=jnp.int32)
    device_id = main_id * subs + lax.axis_index("sub")
    own_count = jnp.sum(jnp.where(device_ids == device_id, counts, 0))[None]
    columns[1], index, bias = lax.optimization_barrier((columns[1], index, bias))
    pieces = gather_rest(columns, "sub")
    main_up = dot(main_in, up_proj)
    groups = [pieces[: len(columns)], pieces[len(columns) :]]
    projected = []
    for group in groups:
        projected.append(project_qkv(down_qkv, group))
    keys = [kv for _, kv in projected]
    keys[-1], out_up = lax.optimization_barrier((keys[-1], out_up))
    out_up = forward(out_up, "sub")
    others = [partner(kv, "main") for kv in keys]
    far = []
    for kv in keys:
        far.append(far_shards(kv, "main"))
    q, stats, acc = near_attention(index, bias, [q for q, _ in projected], keys, others)
    stats, far, *out_up = lax.optimization_barrier((stats, far, *out_up))
    out_ups += [gather_main(part, "main") for part in out_up]
    shards = []
    for k in range(mains // 2 - 1):
        direct = [group[k] for group in far]
        shards += [direct, [partner(part, "main") for part in direct]]
    heads_out = far_attention(index, q, stats, acc, bias, shards)
    own_heads = lax.all_to_all(heads_out.reshape(subs, CAP, heads * HD), "sub", 0, 0)
    span_up, edge_rows = project_up(index, main_up, own_heads, out_ups, own_count)
    previous = lax.ppermute(edge_rows, axes, [(i, i + 1) for i in range(devices - 1)])
    target = span_rank - 1
    spread = (target[:, None] == jnp.arange(CAP)[None, :]).astype(BF)
    inner = (encoded.astype(F32) + dot(spread, span_up)).astype(BF)
    inner, previous = lax.optimization_barrier((inner, previous))
    before = jnp.where((target == -1)[:, None], previous[1][None], previous[0][None])
    outer = (encoded.astype(F32) + before.astype(F32)).astype(BF)
    return jnp.where((target < 0)[:, None], outer, inner)


def solution(mesh):
    return jax.shard_map(
        local,
        mesh=mesh,
        in_specs=(
            P(("main", "sub"), None),
            P(("main", "sub")),
            P(),
            P(),
            P(),
            P(),
            P(),
            P(),
            P(),
            P(),
            P(),
            P(),
            P(),
            P(),
            P(None, "sub", None),
            P("sub", None, None),
            P(),
        ),
        out_specs=P(("main", "sub"), None),
        check_vma=False,
    )
```

```python
import functools
import math

import jax
import jax.numpy as jnp
from jax import lax
from jax.experimental import pallas as pl
from jax.experimental.pallas import tpu as pltpu
from jax.sharding import PartitionSpec as P


INNER_WIDTH = 2048
HEAD_COUNT = 32
HEAD_WIDTH = 64
STATE = 128
HD = 128
CAP = 96
CHUNK = 128
LANES = 128
WITHIN_STEP = 512
STATE_STEP = 1024
FINISH_STEP = 1024
EXTRA = 8

epsilon = 1e-06
highest = lax.Precision.HIGHEST
LOG2E = math.log2(math.e)
BF = jnp.bfloat16
F32 = jnp.float32


def dot(a, b, **kw):
    return jnp.dot(a, b, preferred_element_type=F32, **kw)


def dot_t(a, b):
    return lax.dot_general(a, b, (((1,), (1,)), ((), ())), preferred_element_type=F32)


def silu(v):
    return v * jax.nn.sigmoid(v)


def params(**kw):
    return pltpu.CompilerParams(dimension_semantics=("arbitrary",), **kw)


def cost(us):
    return pl.CostEstimate(flops=int(us * 6e8), transcendentals=0, bytes_accessed=int(us * 3e6))


def whole(shape):
    rank = len(shape)
    return pl.BlockSpec(shape, lambda j: (0,) * rank)


def pair_lanes(columns, pair):
    rows = columns.shape[0]
    low = jnp.broadcast_to(columns[:, 2 * pair : 2 * pair + 1], (rows, LANES))
    high = jnp.broadcast_to(columns[:, 2 * pair + 1 : 2 * pair + 2], (rows, LANES))
    lane = lax.broadcasted_iota(jnp.int32, (rows, LANES), 1)
    return jnp.where(lane < HEAD_WIDTH, low, high)


def padded(row_ref):
    return jnp.concatenate([row_ref[...], jnp.zeros((1, LANES - HEAD_COUNT), F32)], 1)


def step_columns(table, j, width):
    return pltpu.roll(table, (LANES - width // HEAD_WIDTH * j) % LANES, 1)


def states_body(
    bytes_ref, gain_ref, wx_ref, wbc_ref, wdt_ref, bias_ref, rate_ref,
    normed_ref, x_ref, bc_ref, cum_ref, chunk_ref, late_ref, send_ref,
    bt_ref, weight_ref, total_ref,
):
    j = pl.program_id(0)
    rows = bytes_ref.shape[0]
    chunks = rows // CHUNK

    @pl.when(j == 0)
    def _():
        values = bytes_ref[...].astype(F32)
        scale = lax.rsqrt(jnp.mean(values * values, -1, keepdims=True) + epsilon)
        normed = (values * scale * gain_ref[...]).astype(BF)
        normed_ref[...] = normed
        bc = dot(normed, wbc_ref[...])
        bc_ref[...] = bc.astype(BF)
        spare = jnp.zeros((LANES - HEAD_COUNT, normed.shape[1]), BF)
        raw = dot_t(normed, jnp.concatenate([wdt_ref[...], spare], 0)) + padded(bias_ref)
        dt = jnp.maximum(raw, 0.0) + jnp.log1p(jnp.exp(-jnp.abs(raw)))
        step = dt * (-LOG2E * padded(rate_ref))
        row = lax.broadcasted_iota(jnp.int32, (CHUNK, CHUNK), 0)
        col = lax.broadcasted_iota(jnp.int32, (CHUNK, CHUNK), 1)
        lower = (row >= col).astype(F32)
        log_dt = jnp.log(dt) * LOG2E
        end = jnp.zeros((1, LANES), F32)
        lates = []
        for c in range(chunks):
            at = pl.ds(c * CHUNK, CHUNK)
            part = slice(c * CHUNK, (c + 1) * CHUNK)
            within = jnp.dot(lower, step[part], precision=highest, preferred_element_type=F32)
            cum = within + end
            cum_ref[at, :] = cum
            late = cum - log_dt[part]
            lates.append(late)
            turned = late.T
            for quad in range(HEAD_COUNT // 4):
                late_ref[quad, 0:4, at] = turned[4 * quad : 4 * quad + 4]
            end = cum[CHUNK - 1 :, :]
            chunk_ref[at, :] = jnp.exp2(end - late)
            bt_ref[:, at] = bc[part, :STATE].T.astype(BF)
        for c in range(chunks):
            weight_ref[pl.ds(c * CHUNK, CHUNK), :] = jnp.exp2(end - lates[c])
        total_ref[...] = jnp.broadcast_to(jnp.exp2(end), total_ref.shape)

    x = silu(dot(normed_ref[...], wx_ref[...]))
    x_ref[...] = x.astype(BF)
    weight = step_columns(weight_ref[...], j, STATE_STEP)
    factor = step_columns(total_ref[...], j, STATE_STEP)
    spread = jnp.concatenate([pair_lanes(weight, pair) for pair in range(STATE_STEP // LANES)], 1)
    state = dot(bt_ref[...], (x * spread).astype(BF))
    group = send_ref.shape[0] * LANES // STATE_STEP
    piece = send_ref.shape[1] - EXTRA
    for pair in range(STATE_STEP // LANES):
        lanes = slice(pair * LANES, (pair + 1) * LANES)
        decay = pair_lanes(factor, pair)[:1]
        high = decay.astype(BF).astype(F32)
        row = lax.broadcasted_iota(jnp.int32, (EXTRA, LANES), 0)
        tail = jnp.where(row == 0, high, jnp.where(row == 1, decay - high, 0.0)).astype(BF)
        for d in range(group):
            part = slice(d * piece, (d + 1) * piece)
            send_ref[pair * group + d, :piece, :] = state[part, lanes].astype(BF)
            send_ref[pair * group + d, piece:, :] = tail


def scan_states(byte_states, gain, mamba_in, mamba_bc, mamba_dt, bias, rate, devices):
    rows, width = byte_states.shape
    steps = INNER_WIDTH // STATE_STEP
    piece = INNER_WIDTH * STATE // (LANES * devices)
    return pl.pallas_call(
        states_body,
        grid=(steps,),
        in_specs=[
            whole((rows, width)),
            whole((1, width)),
            pl.BlockSpec((width, STATE_STEP), lambda j: (0, j)),
            whole((width, 2 * STATE)),
            whole((HEAD_COUNT, width)),
            whole((1, HEAD_COUNT)),
            whole((1, HEAD_COUNT)),
        ],
        out_specs=[
            whole((rows, width)),
            pl.BlockSpec((rows, STATE_STEP), lambda j: (0, j)),
            whole((rows, 2 * STATE)),
            whole((rows, LANES)),
            whole((rows, LANES)),
            whole((HEAD_COUNT // 4, 8, rows)),
            pl.BlockSpec((devices // steps, piece + EXTRA, LANES), lambda j: (j, 0, 0)),
        ],
        out_shape=[
            jax.ShapeDtypeStruct((rows, width), BF),
            jax.ShapeDtypeStruct((rows, INNER_WIDTH), BF),
            jax.ShapeDtypeStruct((rows, 2 * STATE), BF),
            jax.ShapeDtypeStruct((rows, LANES), F32),
            jax.ShapeDtypeStruct((rows, LANES), F32),
            jax.ShapeDtypeStruct((HEAD_COUNT // 4, 8, rows), F32),
            jax.ShapeDtypeStruct((devices, piece + EXTRA, LANES), BF),
        ],
        scratch_shapes=[
            pltpu.VMEM((STATE, rows), BF),
            pltpu.VMEM((rows, LANES), F32),
            pltpu.VMEM((8, LANES), F32),
        ],
        compiler_params=params(),
        cost_estimate=cost(9),
        name="scan_states",
    )(byte_states, gain, mamba_in, mamba_bc, mamba_dt, bias, rate)


def prefix_body(parts_ref, out_ref):
    devices, piece, _ = out_ref.shape
    state = jnp.zeros((piece, LANES), F32)
    for d in range(devices):
        out_ref[d] = state.astype(BF)
        tail = parts_ref[d, piece:, :].astype(F32)
        decay = tail[0:1] + tail[1:2]
        state = state * decay + parts_ref[d, :piece, :].astype(F32)


def state_prefix(parts):
    devices, rows, _ = parts.shape
    piece = rows - EXTRA
    return pl.pallas_call(
        prefix_body,
        grid=(1,),
        in_specs=[whole(parts.shape)],
        out_specs=whole((devices, piece, LANES)),
        out_shape=jax.ShapeDtypeStruct((devices, piece, LANES), BF),
        compiler_params=params(),
        cost_estimate=cost(2),
        name="state_prefix",
    )(parts)


def within_body(
    normed_ref, wg_ref, x_ref, bc_ref, cum_ref, chunk_ref, late_ref, skip_ref,
    yg_ref, grown_ref, contact_ref, bt_ref,
):
    j = pl.program_id(0)
    rows = normed_ref.shape[0]
    chunks = rows // CHUNK

    @pl.when(j == 0)
    def _():
        row = lax.broadcasted_iota(jnp.int32, (CHUNK, CHUNK), 0)
        col = lax.broadcasted_iota(jnp.int32, (CHUNK, CHUNK), 1)
        for c in range(chunks):
            at = pl.ds(c * CHUNK, CHUNK)
            contact = dot_t(bc_ref[at, STATE:], bc_ref[at, :STATE])
            contact_ref[c] = jnp.where(row >= col, contact, 0.0)
            bt_ref[c] = bc_ref[at, :STATE].astype(F32).T.astype(BF)

    gate = silu(dot(normed_ref[...], wg_ref[...]))
    cum = step_columns(cum_ref[...], j, WITHIN_STEP)
    chunk = step_columns(chunk_ref[...], j, WITHIN_STEP)
    skip = step_columns(jnp.broadcast_to(padded(skip_ref), (8, LANES)), j, WITHIN_STEP)
    lane = lax.broadcasted_iota(jnp.int32, (CHUNK, LANES), 1)
    for pair in range(WITHIN_STEP // LANES):
        lanes = slice(pair * LANES, (pair + 1) * LANES)
        skips = pair_lanes(skip, pair)[:1]
        end = jnp.zeros((1, LANES), F32)
        state = None
        for c in range(chunks):
            at = pl.ds(c * CHUNK, CHUNK)
            part = slice(c * CHUNK, (c + 1) * CHUNK)
            weights = []
            for head in (2 * pair, 2 * pair + 1):
                gap = cum[part, head : head + 1] - late_ref[head // 4, head % 4 : head % 4 + 1, at]
                weights.append((jnp.exp2(jnp.minimum(gap, 126.0)) * contact_ref[c]).astype(BF))
            packed = x_ref[at, lanes]
            zero = jnp.zeros_like(packed)
            stacked = jnp.concatenate(
                [jnp.where(lane < HEAD_WIDTH, packed, zero),
                 jnp.where(lane < HEAD_WIDTH, zero, packed)], 0
            )
            x = packed.astype(F32)
            y = dot(jnp.concatenate(weights, 1), stacked) + skips * x
            spread = pair_lanes(cum[part], pair)
            if c:
                y = y + dot(bc_ref[at, STATE:], state.astype(BF)) * jnp.exp2(spread - end)
            g = gate[part, lanes]
            yg_ref[at, lanes] = (y * g).astype(BF)
            grown_ref[at, lanes] = (jnp.exp2(spread) * g).astype(BF)
            if c + 1 < chunks:
                scaled = (x * pair_lanes(chunk[part], pair)).astype(BF)
                update = dot(bt_ref[c], scaled)
                last = spread[CHUNK - 1 :]
                state = update if c == 0 else state * jnp.exp2(last - end) + update
                end = last


def scan_within(normed, mamba_in, x, bc, cum, chunk, late, skip):
    rows, width = normed.shape
    chunks = rows // CHUNK
    steps = INNER_WIDTH // WITHIN_STEP
    return pl.pallas_call(
        within_body,
        grid=(steps,),
        in_specs=[
            whole((rows, width)),
            pl.BlockSpec((width, WITHIN_STEP), lambda j: (0, j + steps)),
            pl.BlockSpec((rows, WITHIN_STEP), lambda j: (0, j)),
            whole((rows, 2 * STATE)),
            whole((rows, LANES)),
            whole((rows, LANES)),
            pl.BlockSpec((WITHIN_STEP // 256, 8, rows), lambda j: (j, 0, 0)),
            whole((1, HEAD_COUNT)),
        ],
        out_specs=[pl.BlockSpec((rows, WITHIN_STEP), lambda j: (0, j))] * 2,
        out_shape=[jax.ShapeDtypeStruct((rows, INNER_WIDTH), BF)] * 2,
        scratch_shapes=[
            pltpu.VMEM((chunks, CHUNK, CHUNK), F32),
            pltpu.VMEM((chunks, STATE, CHUNK), BF),
        ],
        compiler_params=params(),
        cost_estimate=cost(14),
        name="scan_within",
    )(normed, mamba_in, x, bc, cum, chunk, late, skip)


def finish_body(
    yg_ref, grown_ref, c_ref, incoming_ref, gain_ref, wo_ref, bytes_ref, rank_ref, down_ref,
    encoded_ref, main_ref, sent_ref, acc_ref, square_ref, weight_ref, sem,
):
    j = pl.program_id(0)
    rows = yg_ref.shape[0]

    @pl.when(j == 0)
    def _():
        pltpu.make_async_copy(down_ref, weight_ref, sem).start()
        square_ref[...] = jnp.zeros_like(square_ref)

    state = jnp.concatenate([incoming_ref[p] for p in range(incoming_ref.shape[0])], 1)
    carried = dot(c_ref[...], state)
    gated = yg_ref[...].astype(F32) + carried * grown_ref[...].astype(F32)
    parts = [gated[:, p : p + LANES] for p in range(0, FINISH_STEP, LANES)]
    square_ref[...] += sum(part * part for part in parts)
    mixed = dot((gated * gain_ref[...]).astype(BF), wo_ref[...])

    @pl.when(j == 0)
    def _():
        acc_ref[...] = mixed

    @pl.when(j > 0)
    def _():
        acc_ref[...] += mixed

    @pl.when(j == pl.num_programs(0) - 1)
    def _():
        mean = jnp.sum(square_ref[...], -1, keepdims=True) * (1.0 / INNER_WIDTH)
        encoded = (bytes_ref[...].astype(F32) + acc_ref[...] * lax.rsqrt(mean + epsilon)).astype(BF)
        encoded_ref[...] = encoded
        slot = lax.broadcasted_iota(jnp.int32, (CAP, rows), 0)
        picker = jnp.where(rank_ref[...] == slot, 1.0, 0.0).astype(BF)
        spans = dot(picker, encoded)
        pltpu.make_async_copy(down_ref, weight_ref, sem).wait()
        main_in = dot(spans.astype(BF), weight_ref[...]).astype(BF)
        main_ref[...] = main_in
        wide = main_in.astype(F32)
        scale = lax.rsqrt(jnp.mean(wide * wide, -1, keepdims=True) + epsilon)
        sent_ref[...] = (spans * scale).astype(BF)


def scan_finish(yg, grown, bc, incoming, gain, mamba_out, byte_states, rank, down):
    rows, width = byte_states.shape
    steps = INNER_WIDTH // FINISH_STEP
    return pl.pallas_call(
        finish_body,
        grid=(steps,),
        in_specs=[
            pl.BlockSpec((rows, FINISH_STEP), lambda j: (0, j)),
            pl.BlockSpec((rows, FINISH_STEP), lambda j: (0, j)),
            pl.BlockSpec((rows, STATE), lambda j: (0, 1)),
            pl.BlockSpec((FINISH_STEP // LANES, STATE, LANES), lambda j: (j, 0, 0)),
            pl.BlockSpec((1, FINISH_STEP), lambda j: (0, j)),
            pl.BlockSpec((FINISH_STEP, width), lambda j: (j, 0)),
            whole((rows, width)),
            whole((1, rows)),
            pl.BlockSpec(memory_space=pl.ANY),
        ],
        out_specs=[whole((rows, width)), whole((CAP, down.shape[1])), whole((CAP, width))],
        out_shape=[
            jax.ShapeDtypeStruct((rows, width), BF),
            jax.ShapeDtypeStruct((CAP, down.shape[1]), BF),
            jax.ShapeDtypeStruct((CAP, width), BF),
        ],
        scratch_shapes=[
            pltpu.VMEM((rows, width), F32),
            pltpu.VMEM((rows, LANES), F32),
            pltpu.VMEM(down.shape, BF),
            pltpu.SemaphoreType.DMA(()),
        ],
        compiler_params=params(),
        cost_estimate=cost(10),
        name="scan_finish",
    )(yg, grown, bc, incoming, gain, mamba_out, byte_states, rank, down)


def sub_grid(count):
    minor = 1
    while minor * minor * 4 <= count:
        minor *= 2
    return count // minor, minor


def sub_move(value, axis, dz, dx):
    count = lax.axis_size(axis)
    major, minor = sub_grid(count)
    route = []
    for i in range(count):
        z, x = divmod(i, minor)
        route.append((i, (z + dz) % major * minor + (x + dx) % minor))
    return lax.ppermute(value, axis, route)


def places(major):
    return [0, 1, major - 1] + list(range(2, major - 1))


def gather_columns(block, axis):
    major, _ = sub_grid(lax.axis_size(axis))
    *near, last = places(major)
    near = [block] + [sub_move(block, axis, dz, 0) for dz in near[1:]]
    return near + [sub_move(block, axis, last, 0)]


def forward(value, axis):
    _, minor = sub_grid(lax.axis_size(axis))
    return [sub_move(value, axis, 0, dx) for dx in range(1, minor)]


def gather_rest(columns, axis):
    moved = [forward(c, axis) for c in columns]
    return columns + [piece for dx in zip(*moved) for piece in dx]


def sub_sources(axis):
    count = lax.axis_size(axis)
    major, minor = sub_grid(count)
    me = lax.axis_index(axis)
    z, x = me // minor, me % minor
    return [(z - dz) % major * minor + (x - dx) % minor
            for dx in range(minor) for dz in places(major)]


def partner(value, axis):
    count = lax.axis_size(axis)
    return lax.ppermute(value, axis, [(i, i ^ 1) for i in range(count)])


def gather_main(block, axis):
    count = lax.axis_size(axis)
    near = [block] + [
        lax.ppermute(block, axis, [(i, (i + k) % count) for i in range(count)])
        for k in range(2, count, 2)
    ]
    return near + [partner(part, axis) for part in near]


def main_sources(axis):
    count = lax.axis_size(axis)
    me = lax.axis_index(axis)
    return [(m - k) % count for m in (me, me ^ 1) for k in range(0, count, 2)]


def qkv_body(weight_ref, *refs):
    *pieces, q_ref, kv_ref = refs
    rows = jnp.concatenate([piece[...] for piece in pieces], 0)
    for h in range(weight_ref.shape[1] // (3 * HD)):
        out = dot(rows, weight_ref[:, h * 3 * HD : (h + 1) * 3 * HD])
        q_ref[:, h * HD : (h + 1) * HD] = (out[:, :HD] * (HD**-0.5 * LOG2E)).astype(BF)
        kv_ref[:, h * 2 * HD : (h + 1) * 2 * HD] = out[:, HD:].astype(BF)


def vmem(count):
    return [pl.BlockSpec(memory_space=pltpu.VMEM)] * count


SCALARS = pl.BlockSpec(memory_space=pltpu.SMEM)


def project_qkv(weight, pieces):
    slots = pieces[0].shape[0] * len(pieces)
    heads = weight.shape[1] // (3 * HD)
    return pl.pallas_call(
        qkv_body,
        in_specs=vmem(1 + len(pieces)),
        out_specs=vmem(2),
        out_shape=[
            jax.ShapeDtypeStruct((slots, heads * HD), BF),
            jax.ShapeDtypeStruct((slots, heads * 2 * HD), BF),
        ],
        cost_estimate=cost(4),
        name="project_qkv",
    )(weight, *pieces)


def place(out_ref, index_ref, parts):
    first = index_ref.shape[0] - out_ref.shape[0] // CAP
    for part in parts:
        for p in range(part.shape[0] // CAP):
            at = pl.multiple_of(index_ref[first] * CAP, 32)
            out_ref[pl.ds(at, CAP), :] = part[p * CAP : (p + 1) * CAP, :]
            first += 1


def span_up_body(index_ref, edge_ref, main_up_ref, heads_ref, *refs):
    *weights, up_ref, edges_ref, columns_ref = refs
    subs, cap, _ = heads_ref.shape
    mains = columns_ref.shape[0]
    depth = weights[0].shape[0]
    flat = jnp.concatenate([heads_ref[index_ref[1 + mains + r]] for r in range(subs)], 1)
    for p in range(mains):
        part = 0.0
        for g, weight in enumerate(weights[p::mains]):
            part = part + dot(flat[:, g * depth : (g + 1) * depth], weight[...])
        columns_ref[index_ref[1 + p]] = part
    joined = jnp.concatenate([columns_ref[p] for p in range(mains)], 1)
    up = (main_up_ref[...] + joined).astype(BF)
    up_ref[...] = up
    slot = lax.broadcasted_iota(jnp.int32, (16, cap), 1)
    row = lax.broadcasted_iota(jnp.int32, (16, cap), 0)
    picker = jnp.where((slot == edge_ref[0] - 2 + row) & (row < 2), 1.0, 0.0).astype(BF)
    edges_ref[...] = dot(picker, up).astype(BF)


def project_up(index, main_up, heads, groups, own_count):
    cap, width = main_up.shape
    part = groups[0][0].shape[1]
    weights = [weight for group in groups for weight in group]
    return pl.pallas_call(
        span_up_body,
        in_specs=[SCALARS, SCALARS] + vmem(2 + len(weights)),
        out_specs=vmem(2),
        out_shape=[
            jax.ShapeDtypeStruct((cap, width), BF),
            jax.ShapeDtypeStruct((16, width), BF),
        ],
        scratch_shapes=[pltpu.VMEM((len(groups[0]), cap, part), F32)],
        cost_estimate=cost(5),
        name="project_up",
    )(index, own_count, main_up, heads, *weights)


BLOCK = 384


def scores_of(q, kv_ref, bias, head, span):
    return dot_t(q, kv_ref[:span, head * 2 * HD : head * 2 * HD + HD]) + bias[:, :span]


def mixed_of(numer, kv_ref, head, span):
    return dot(numer.astype(BF), kv_ref[:span, head * 2 * HD + HD : (head + 1) * 2 * HD])


def join(carry, q, kv_refs, biases, head):
    top, total, acc = carry
    slots = kv_refs[0].shape[0]
    scores = [scores_of(q, kv, bias, head, slots) for kv, bias in zip(kv_refs, biases)]
    new = top
    for s in scores:
        new = jnp.maximum(new, jnp.max(s, -1, keepdims=True))
    rescale = jnp.exp2(top - new)
    total, acc = total * rescale, acc * rescale
    for s, kv in zip(scores, kv_refs):
        numer = jnp.exp2(s - new)
        total = total + jnp.sum(numer, -1, keepdims=True)
        acc = acc + mixed_of(numer, kv, head, slots)
    return new, total, acc


def store(stats_ref, acc_ref, at, head, carry):
    top, total, acc = carry
    acc_ref[at, head * HD : (head + 1) * HD] = acc
    stats_ref[2 * head, at, :] = jnp.broadcast_to(top, acc.shape)
    stats_ref[2 * head + 1, at, :] = jnp.broadcast_to(total, acc.shape)


def near_body(index_ref, bias_ref, *refs):
    *parts, q_ref, stats_ref, acc_ref, kv_ref, other_ref = refs
    count = len(parts) // 3
    place(q_ref, index_ref, parts[:count])
    place(kv_ref, index_ref, parts[count : 2 * count])
    pl.when(index_ref[0] % 2 == 1)(lambda: place(other_ref, index_ref, parts[2 * count :]))
    slots = q_ref.shape[0]
    heads = q_ref.shape[1] // HD
    mine = index_ref[0]

    def own(at, b, head):
        span = (b + 1) * BLOCK
        q = q_ref[at, head * HD : (head + 1) * HD]
        scores = scores_of(q, kv_ref, bias_ref[mine], head, span)
        row = lax.broadcasted_iota(jnp.int32, scores.shape, 0) + b * BLOCK
        col = lax.broadcasted_iota(jnp.int32, scores.shape, 1)
        scores = jnp.where(col <= row, scores, -2e30)
        top = jnp.max(scores, -1, keepdims=True)
        numer = jnp.exp2(scores - top)
        return top, jnp.sum(numer, -1, keepdims=True), mixed_of(numer, kv_ref, head, span)

    def run(paired):
        for b in range(slots // BLOCK):
            at = pl.ds(b * BLOCK, BLOCK)
            for head in range(heads):
                carry = own(at, b, head)
                if paired:
                    q = q_ref[at, head * HD : (head + 1) * HD]
                    carry = join(carry, q, [other_ref], [bias_ref[mine - 1]], head)
                store(stats_ref, acc_ref, at, head, carry)

    pl.when(mine % 2 == 1)(lambda: run(True))
    pl.when(mine % 2 == 0)(lambda: run(False))


def near_attention(index, bias, queries, keys, others):
    slots = bias.shape[2]
    width = queries[0].shape[1]
    parts = [*queries, *keys, *others]
    return pl.pallas_call(
        near_body,
        in_specs=[SCALARS] + vmem(1 + len(parts)),
        out_specs=vmem(3),
        out_shape=[
            jax.ShapeDtypeStruct((slots, width), BF),
            jax.ShapeDtypeStruct((2 * width // HD, slots, HD), F32),
            jax.ShapeDtypeStruct((slots, width), F32),
        ],
        scratch_shapes=[pltpu.VMEM((slots, 2 * width), BF)] * 2,
        cost_estimate=cost(9),
        name="near_attention",
    )(index, bias, *parts)


def far_body(index_ref, q_ref, stats_in, acc_in, bias_ref, *refs, shards):
    parts, (out_ref, stats_ref, acc_ref, *pieces) = refs[: -3 - shards], refs[-3 - shards :]
    slots = q_ref.shape[0]
    heads = q_ref.shape[1] // HD
    mine = index_ref[0]
    steps = shards // 2
    count = len(parts) // shards

    @pl.when(mine >= 2)
    def _():
        for p, piece in enumerate(pieces):
            place(piece, index_ref, parts[p * count : (p + 1) * count])

    def finish(at, head, carry):
        out_ref[at, head * HD : (head + 1) * HD] = (carry[2] / carry[1]).astype(BF)

    def each(refs, act):
        for b in range(slots // BLOCK):
            at = pl.ds(b * BLOCK, BLOCK)
            for head in range(heads):
                acc = refs[1][at, head * HD : (head + 1) * HD]
                act(at, head, (refs[0][2 * head, at, :1], refs[0][2 * head + 1, at, :1], acc))

    for k in range(steps):
        def act(at, head, carry, k=k):
            sources = (mine - 2 * (k + 1), mine + 1 - 2 * (mine % 2) - 2 * (k + 1))
            q = q_ref[at, head * HD : (head + 1) * HD]
            biases = [bias_ref[source] for source in sources]
            carry = join(carry, q, pieces[2 * k : 2 * k + 2], biases, head)
            last = mine < 2 * (k + 2)
            if k + 1 == steps:
                finish(at, head, carry)
            else:
                pl.when(last)(lambda: finish(at, head, carry))
                pl.when(jnp.logical_not(last))(lambda: store(stats_ref, acc_ref, at, head, carry))

        source_refs = (stats_in, acc_in) if k == 0 else (stats_ref, acc_ref)
        pl.when(mine >= 2 * (k + 1))(functools.partial(each, source_refs, act))

    pl.when(mine < 2)(functools.partial(each, (stats_in, acc_in), finish))


def far_attention(index, q, stats, acc, bias, shards):
    slots, width = q.shape
    parts = [part for shard in shards for part in shard]
    return pl.pallas_call(
        functools.partial(far_body, shards=len(shards)),
        in_specs=[SCALARS] + vmem(4 + len(parts)),
        out_specs=vmem(1)[0],
        out_shape=jax.ShapeDtypeStruct((slots, width), BF),
        scratch_shapes=[pltpu.VMEM(stats.shape, F32), pltpu.VMEM((slots, width), F32)]
        + [pltpu.VMEM((slots, 2 * width), BF)] * len(shards),
        cost_estimate=cost(9),
        name="far_attention",
    )(index, q, stats, acc, bias, *parts)


def far_shards(kv, axis):
    count = lax.axis_size(axis)
    shifts = range(2, count, 2)
    return [lax.ppermute(kv, axis, [(i - k, i) for i in range(k, count)]) for k in shifts]


def local(
    byte_states,
    boundary_flags,
    span_counts,
    enc_norm_gain,
    mamba_in,
    mamba_bc,
    mamba_dt,
    dt_bias,
    decay_rate,
    skip_gain,
    gate_norm_gain,
    mamba_out,
    down_proj,
    attn_norm_gain,
    qkv_weight,
    out_weight,
    up_proj,
):
    axes = ("main", "sub")
    devices = lax.axis_size(axes)
    subs = lax.axis_size("sub")
    mains = lax.axis_size("main")
    main_id = lax.axis_index("main")
    _, width = byte_states.shape
    heads = qkv_weight.shape[1]
    model = qkv_weight.shape[0]

    normed, x, bc, cum, chunk, late, send = scan_states(
        byte_states,
        enc_norm_gain[None],
        mamba_in,
        mamba_bc,
        mamba_dt.T,
        dt_bias[None],
        decay_rate[None],
        devices,
    )
    send, weight, up, out, main_id = lax.optimization_barrier(
        (send, qkv_weight, up_proj, out_weight, main_id)
    )
    parts = lax.all_to_all(send, axes, 0, 0, tiled=True)
    weight = weight.reshape(model, -1)
    up_part = width // mains
    up_columns = lax.dynamic_slice_in_dim(up, main_id * up_part, up_part, 1)
    out_up = dot(out.reshape(heads * HD, model), up_columns).astype(BF)
    yg, grown = scan_within(normed, mamba_in, x, bc, cum, chunk, late, skip_gain[None])
    parts, yg, grown, down, weight, flags, out_up = lax.optimization_barrier(
        (parts, yg, grown, down_proj, weight, boundary_flags, out_up)
    )
    incoming = lax.all_to_all(state_prefix(parts), axes, 0, 0, tiled=True)
    incoming = incoming.reshape(HEAD_COUNT // 2, STATE, LANES)
    scaled_down = (down.astype(F32) * attn_norm_gain[None]).astype(BF)
    down_qkv = dot(scaled_down, weight).astype(BF)
    span_rank = jnp.cumsum(flags) - 1
    picked = jnp.where(flags == 1, span_rank, -1)
    incoming, down_qkv, picked, out_up = lax.optimization_barrier(
        (incoming, down_qkv, picked, out_up)
    )
    out_up = gather_columns(out_up, "sub")

    encoded, main_in, sent_rows = scan_finish(
        yg,
        grown,
        bc,
        incoming,
        gate_norm_gain[None],
        mamba_out,
        byte_states,
        picked[None],
        down_proj,
    )
    sent_rows, counts, main_id, *out_up = lax.optimization_barrier(
        (sent_rows, span_counts, main_id, *out_up)
    )
    out_up = jnp.concatenate(out_up, 0)
    out_ups = [gather_main(out_up, "main")]
    columns = gather_columns(sent_rows, "sub")
    sub_index = sub_sources("sub")
    major = len(columns)
    early = [p for p in range(subs) if p < major - 1 or (p >= major and p % major == 0)]
    order = early + [p for p in range(subs) if p not in early]
    index = [main_id] + main_sources("main") + sub_index + [sub_index[p] for p in order]
    index = jnp.stack(index).astype(jnp.int32)
    slot = jnp.arange(subs * CAP, dtype=jnp.int32)
    valid = slot[None] % CAP < jnp.repeat(counts.reshape(mains, subs), CAP, axis=1)
    bias = jnp.where(valid, 0.0, -1e30).astype(F32)[:, None, :]
    device_ids = jnp.arange(devices, dtype=jnp.int32)
    device_id = main_id * subs + lax.axis_index("sub")
    own_count = jnp.sum(jnp.where(device_ids == device_id, counts, 0))[None]
    columns[1], index, bias = lax.optimization_barrier((columns[1], index, bias))
    pieces = gather_rest(columns, "sub")
    main_up = dot(main_in, up_proj)
    pieces = [pieces[p] for p in order]
    groups = [pieces[: len(early)], pieces[len(early) :]]
    projected = []
    for group in groups:
        projected.append(project_qkv(down_qkv, group))
    keys = [kv for _, kv in projected]
    keys[-1], out_up = lax.optimization_barrier((keys[-1], out_up))
    out_up = forward(out_up, "sub")
    others = [partner(kv, "main") for kv in keys]
    far = []
    for kv in keys:
        far.append(far_shards(kv, "main"))
    q, stats, acc = near_attention(index, bias, [q for q, _ in projected], keys, others)
    out_up = lax.optimization_barrier((far, out_up))[1]
    stats, far = lax.optimization_barrier((stats, far))
    out_ups += [gather_main(part, "main") for part in out_up]
    shards = []
    for k in range(mains // 2 - 1):
        direct = [group[k] for group in far]
        shards += [direct, [partner(part, "main") for part in direct]]
    heads_out = far_attention(index, q, stats, acc, bias, shards)
    own_heads = lax.all_to_all(heads_out.reshape(subs, CAP, heads * HD), "sub", 0, 0)
    span_up, edge_rows = project_up(index, main_up, own_heads, out_ups, own_count)
    previous = lax.ppermute(edge_rows, axes, [(i, i + 1) for i in range(devices - 1)])
    target = span_rank - 1
    spread = (target[:, None] == jnp.arange(CAP)[None, :]).astype(BF)
    inner = (encoded.astype(F32) + dot(spread, span_up)).astype(BF)
    inner, previous = lax.optimization_barrier((inner, previous))
    before = jnp.where((target == -1)[:, None], previous[1][None], previous[0][None])
    outer = (encoded.astype(F32) + before.astype(F32)).astype(BF)
    return jnp.where((target < 0)[:, None], outer, inner)


def solution(mesh):
    return jax.shard_map(
        local,
        mesh=mesh,
        in_specs=(
            P(("main", "sub"), None),
            P(("main", "sub")),
            P(),
            P(),
            P(),
            P(),
            P(),
            P(),
            P(),
            P(),
            P(),
            P(),
            P(),
            P(),
            P(None, "sub", None),
            P("sub", None, None),
            P(),
        ),
        out_specs=P(("main", "sub"), None),
        check_vma=False,
    )
```
